256 devices in a mesh: batch: 128 (over y, z, x), tile: 2 (over core).
Axes of the slice: x: 4, y: 4, z: 8, core: 2. Of those that a mesh axis runs over, the one named last changes fastest.
Arguments:
- first_view: bfloat16 [256, 8192], P('batch'), may hold values from -1500 to 1500
- second_view: bfloat16 [256, 8192], P('batch'), may hold values from -1500 to 1500
Outputs:
- grad_first: bfloat16 [256, 8192], P('batch', 'tile')
- grad_second: bfloat16 [256, 8192], P('batch', 'tile')
The draws below stay inside these ranges and needn't reach their ends.
All inputs are finite; a program needn't handle non-finite values.
Results may differ from the reference program's by a relative error of at most 0.0043.
Values may be sent and summed in bfloat16 or wider, within the bound.
A program may use at most 64 MiB of HBM per device.

```python
import math
import jax
import jax.numpy as jnp
from jax import lax

D = 8192
BATCH = 256


def view_pair(key):
    keys = jax.random.split(jax.random.fold_in(key, 11), 10)
    shared = jax.random.truncated_normal(keys[0], -4.0, 4.0, (BATCH, 1), jnp.float32)
    noise_one = jax.random.truncated_normal(keys[1], -4.0, 4.0, (BATCH, D), jnp.float32)
    noise_two = jax.random.truncated_normal(keys[2], -4.0, 4.0, (BATCH, D), jnp.float32)
    rise = math.log(10.0)
    place = jnp.arange(BATCH, dtype=jnp.float32) / BATCH
    row_scale = jnp.exp(rise * place[:, None] + jax.random.uniform(keys[3], (BATCH, 1), jnp.float32, -0.35, 0.35))
    load_one = jax.random.uniform(keys[4], (1, D), jnp.float32, 0.15, 0.45)
    load_two = jax.random.uniform(keys[5], (1, D), jnp.float32, 0.15, 0.45)
    scale_one = jnp.exp(jax.random.uniform(keys[6], (1, D), jnp.float32, 0.0, math.log(10.0)))
    scale_two = jnp.exp(jax.random.uniform(keys[7], (1, D), jnp.float32, 0.0, math.log(10.0)))
    offset_one = jax.random.uniform(keys[8], (1, D), jnp.float32, -2.0, 2.0)
    offset_two = jax.random.uniform(keys[9], (1, D), jnp.float32, -2.0, 2.0)
    first = scale_one * (offset_one + row_scale * (load_one * shared + noise_one))
    second = scale_two * (offset_two + row_scale * (load_two * shared + 0.6 * noise_one + 0.8 * noise_two))
    return (first, second)


def draw_first_view(key, part):
    first, second = view_pair(key)
    return first.astype(jnp.bfloat16)


def draw_second_view(key, part):
    first, second = view_pair(key)
    return second.astype(jnp.bfloat16)


def setup_inputs(seed: int = 0) -> dict:
    seeds = jax.random.split(jax.random.key(seed), 3)
    return {
        "first_view": draw_first_view(jax.random.fold_in(seeds[2], 71), 0),
        "second_view": draw_second_view(jax.random.fold_in(seeds[2], 71), 0),
    }


epsilon = 1e-05
decorrelation = 0.0051

def normalized(view, total_rows):
    values = view.astype(jnp.float32)
    mean_value = lax.optimization_barrier(jnp.sum(values, 0)) / total_rows
    variance = lax.optimization_barrier(jnp.sum(values * values, 0)) / total_rows - mean_value * mean_value
    inverse = lax.rsqrt(variance + epsilon)
    return (((values - mean_value) * inverse).astype(jnp.bfloat16), inverse)

def reference(first_view, second_view):
    total_rows, feature_width = first_view.shape
    norm_first, inverse_first = normalized(first_view, total_rows)
    norm_second, inverse_second = normalized(second_view, total_rows)
    block_width = math.gcd(feature_width, 512)
    block_count = feature_width // block_width
    first_blocks = norm_first.reshape(total_rows, block_count, block_width).transpose(1, 0, 2)

    def step_block(carry, inputs):
        pull_second, stat_second = carry
        first_block, block_index = inputs
        correlation = lax.dot_general(first_block, norm_second, (((0,), (0,)), ((), ())), preferred_element_type=jnp.float32) / total_rows
        row_ids = block_index * block_width + lax.iota(jnp.int32, block_width)
        col_ids = lax.iota(jnp.int32, feature_width)
        diagonal = row_ids[:, None] == col_ids[None, :]
        slope_tile = jnp.where(diagonal, correlation - 1.0, decorrelation * correlation).astype(jnp.bfloat16)
        weighted = slope_tile.astype(jnp.float32) * correlation
        pull_block = lax.dot_general(norm_second, slope_tile, (((1,), (1,)), ((), ())), preferred_element_type=jnp.float32)
        pull_second = pull_second + jnp.dot(first_block, slope_tile, preferred_element_type=jnp.float32)
        stat_second = stat_second + lax.optimization_barrier(jnp.sum(weighted, 0))
        return ((pull_second, stat_second), (pull_block, lax.optimization_barrier(jnp.sum(weighted, 1))))
    start_carry = (jnp.zeros((total_rows, feature_width), jnp.float32), jnp.zeros((feature_width,), jnp.float32))
    indices = jnp.arange(block_count, dtype=jnp.int32)
    (pull_second, stat_second), (pull_blocks, stat_blocks) = lax.scan(step_block, start_carry, (first_blocks, indices))
    pull_first = pull_blocks.transpose(1, 0, 2).reshape(total_rows, feature_width)
    stat_first = stat_blocks.reshape(feature_width)
    grad_first = (inverse_first * (pull_first - norm_first.astype(jnp.float32) * stat_first)).astype(jnp.bfloat16)
    grad_second = (inverse_second * (pull_second - norm_second.astype(jnp.float32) * stat_second)).astype(jnp.bfloat16)
    return (grad_first, grad_second)
```

```python
import functools

import jax
import jax.numpy as jnp
from jax import lax
from jax.experimental import pallas as pl
from jax.experimental.pallas import tpu as pltpu
from jax.sharding import PartitionSpec as P

epsilon = 1e-05
decorrelation = 0.0051

NY, NZ, NX = 4, 8, 4
PLANE = NY * NX
MESH = pl.DeviceIdType.MESH


def kernel(
    first_ref,
    second_ref,
    grad_first_ref,
    grad_second_ref,
    piece,
    line,
    whole,
    norm,
    gram_out,
    gram_in,
    core_out,
    core_in,
    stat_out,
    stat_in,
    grad_out,
    send_sem,
    recv_sem,
):
    batch = lax.axis_index("batch")
    tile = lax.axis_index("tile")
    x = batch % NX
    z = (batch // NX) % NZ
    y = batch // (NX * NZ)
    slot = y * NX + x
    width = piece.shape[-1]
    half = width * NZ
    rows = line.shape[1]
    total_rows = rows * PLANE

    def line_peer(k):
        other = (z + k) % NZ
        return other, ((y * NZ + other) * NX + x, tile)

    def plane_peer(j, i):
        return ((((y + j) % NY) * NZ + z) * NX + (x + i) % NX, tile)

    line_steps = [4, 3, 5, 2, 6, 1, 7]
    plane_steps = [(j, i) for j in (2, 1, 3, 0) for i in (2, 1, 3, 0) if i or j]
    sibling = (batch, 1 - tile)

    barrier = pltpu.get_barrier_semaphore()
    for k in line_steps:
        pl.semaphore_signal(barrier, inc=1, device_id=line_peer(k)[1], device_id_type=MESH)
    for j, i in plane_steps:
        pl.semaphore_signal(barrier, inc=1, device_id=plane_peer(j, i), device_id_type=MESH)
    pl.semaphore_signal(barrier, inc=1, device_id=sibling, device_id_type=MESH)
    pl.semaphore_wait(barrier, len(line_steps) + len(plane_steps) + 1)

    def send(phase, source, target, device):
        pltpu.make_async_remote_copy(
            src_ref=source,
            dst_ref=target,
            send_sem=send_sem.at[phase],
            recv_sem=recv_sem.at[phase],
            device_id=device,
            device_id_type=MESH,
        ).start()

    def wait(sems, phase, like):
        pltpu.make_async_copy(like, like, sems.at[phase]).wait()

    views = (first_ref, second_ref)
    for k in line_steps:
        other, device = line_peer(k)
        start = pl.multiple_of(tile * half + other * width, width)
        for v in range(2):
            send(0, views[v].at[:, pl.ds(start, width)], piece.at[z, v], device)
    start = pl.multiple_of(tile * half + z * width, width)
    for v in range(2):
        pltpu.make_async_copy(
            views[v].at[:, pl.ds(start, width)], piece.at[z, v], recv_sem.at[0]
        ).start()
    wait(recv_sem, 0, piece)
    for v in range(2):
        line[v] = piece[:, v].astype(jnp.float32).reshape(rows, width).astype(jnp.bfloat16)

    for j, i in plane_steps:
        send(1, line, whole.at[slot], plane_peer(j, i))
    whole[slot] = line[...]
    wait(recv_sem, 1, whole.at[pl.ds(0, PLANE - 1)])

    inverse = []
    for v in range(2):
        values = whole[:, v].astype(jnp.float32).reshape(total_rows, width)
        mean = jnp.sum(values, 0, keepdims=True) / total_rows
        centered = values - mean
        variance = jnp.sum(centered * centered, 0, keepdims=True) / total_rows
        inverse.append(lax.rsqrt(variance + epsilon))
        norm[v] = (centered * inverse[v]).astype(jnp.bfloat16).reshape(PLANE, rows, width)
    for v in range(2):
        gram_out[v] = lax.dot_general(
            norm[v, slot],
            norm[v].reshape(total_rows, width),
            (((1,), (1,)), ((), ())),
            preferred_element_type=jnp.float32,
        ).astype(jnp.bfloat16)

    for k in line_steps:
        send(2, gram_out, gram_in.at[z], line_peer(k)[1])
    gram_in[z] = gram_out[...]
    norm_first = norm[0].reshape(total_rows, width)
    norm_second = norm[1].reshape(total_rows, width)
    paired = (
        jnp.sum(norm_first.astype(jnp.float32) * norm_second.astype(jnp.float32), 0, keepdims=True)
        / total_rows
    )
    excess = (paired - 1.0) - decorrelation * paired
    wait(recv_sem, 2, gram_in.at[pl.ds(0, NZ - 1)])
    core_out[...] = jnp.sum(gram_in[...].astype(jnp.float32), 0)

    send(3, core_out, core_in, sibling)
    wait(recv_sem, 3, core_in)
    gram = (core_out[...] + core_in[...]) * (decorrelation / total_rows)

    pulls = []
    mine = [norm[v, slot].astype(jnp.float32) for v in range(2)]
    for v in range(2):
        high = gram[1 - v].astype(jnp.bfloat16)
        low = (gram[1 - v] - high.astype(jnp.float32)).astype(jnp.bfloat16)
        both = jnp.dot(
            jnp.concatenate([high, low], 0),
            (norm_first, norm_second)[v],
            preferred_element_type=jnp.float32,
        )
        pull = both[:rows] + both[rows:] + excess * mine[1 - v]
        pulls.append(pull)
        stat_out[v : v + 1] = jnp.sum(pull * mine[v], 0, keepdims=True)

    for j, i in plane_steps:
        send(4, stat_out, stat_in.at[slot], plane_peer(j, i))
    stat_in[slot] = stat_out[...]
    wait(recv_sem, 4, stat_in.at[pl.ds(0, PLANE - 1)])
    stat = jnp.sum(stat_in[...], 0) / total_rows
    for v in range(2):
        grad = inverse[v] * (pulls[v] - mine[v] * stat[v : v + 1])
        grad_out[:, v] = grad.reshape(NZ, rows // NZ, width).astype(jnp.bfloat16)

    grads = (grad_first_ref, grad_second_ref)
    start = pl.multiple_of(z * width, width)
    for k in line_steps:
        other, device = line_peer(k)
        for v in range(2):
            send(5 + v, grad_out.at[other, v], grads[v].at[:, pl.ds(start, width)], device)
    for v in range(2):
        pltpu.make_async_copy(
            grad_out.at[z, v], grads[v].at[:, pl.ds(start, width)], recv_sem.at[5 + v]
        ).start()
    for v in range(2):
        wait(recv_sem, 5 + v, grads[v])

    wait(send_sem, 0, piece.at[pl.ds(0, NZ - 1)])
    wait(send_sem, 1, whole.at[pl.ds(0, PLANE - 1)])
    wait(send_sem, 2, gram_in.at[pl.ds(0, NZ - 1)])
    wait(send_sem, 3, core_in)
    wait(send_sem, 4, stat_in.at[pl.ds(0, PLANE - 1)])
    for v in range(2):
        wait(send_sem, 5 + v, grad_out.at[pl.ds(0, NZ - 1), v])


def per_device(first_view, second_view):
    row_count, feature_width = first_view.shape
    half = feature_width // 2
    width = half // NZ
    rows = row_count * NZ
    total_rows = rows * PLANE
    bf16, f32 = jnp.bfloat16, jnp.float32
    out = jax.ShapeDtypeStruct((row_count, half), bf16)
    return pl.pallas_call(
        kernel,
        out_shape=(out, out),
        in_specs=[pl.BlockSpec(memory_space=pltpu.VMEM)] * 2,
        out_specs=(pl.BlockSpec(memory_space=pltpu.VMEM),) * 2,
        scratch_shapes=[
            pltpu.VMEM((NZ, 2, row_count, width), bf16),
            pltpu.VMEM((2, rows, width), bf16),
            pltpu.VMEM((PLANE, 2, rows, width), bf16),
            pltpu.VMEM((2, PLANE, rows, width), bf16),
            pltpu.VMEM((2, rows, total_rows), bf16),
            pltpu.VMEM((NZ, 2, rows, total_rows), bf16),
            pltpu.VMEM((2, rows, total_rows), f32),
            pltpu.VMEM((2, rows, total_rows), f32),
            pltpu.VMEM((2, width), f32),
            pltpu.VMEM((PLANE, 2, width), f32),
            pltpu.VMEM((NZ, 2, row_count, width), bf16),
            pltpu.SemaphoreType.DMA((7,)),
            pltpu.SemaphoreType.DMA((7,)),
        ],
        compiler_params=pltpu.CompilerParams(
            collective_id=0, has_side_effects=True, vmem_limit_bytes=32 << 20
        ),
        name="twins",
    )(first_view, second_view)


def solution(mesh):
    return jax.shard_map(
        per_device,
        mesh=mesh,
        in_specs=(P("batch", None), P("batch", None)),
        out_specs=(P("batch", "tile"), P("batch", "tile")),
        check_vma=False,
    )
```

```python
import jax
import jax.numpy as jnp
from jax import lax
from jax.experimental import pallas as pl
from jax.experimental.pallas import tpu as pltpu
from jax.sharding import PartitionSpec as P

epsilon = 1e-05
decorrelation = 0.0051

NY, NZ, NX = 4, 8, 4
PLANE = NY * NX
CORES = 2
LANES = 128
MESH = pl.DeviceIdType.MESH


def kernel(
    first_ref,
    second_ref,
    grads_ref,
    stage,
    line,
    whole,
    norm,
    other,
    gram_out,
    gram_in,
    stat_out,
    stat_in,
    grad_out,
    load_sem,
    line_sem,
    send_sem,
    recv_sem,
):
    batch = lax.axis_index("batch")
    tile = lax.axis_index("tile")
    x = batch % NX
    z = (batch // NX) % NZ
    y = batch // (NX * NZ)
    slot = y * NX + x
    chunks, pair = line.shape[0], line.shape[2]
    rows = NZ * pair
    total_rows = rows * PLANE
    whole_rows = whole.reshape(PLANE, chunks, rows, LANES)
    grad_rows = grad_out.reshape(chunks, rows, LANES)

    def line_peer(k):
        return (y * NZ + (z + k) % NZ) * NX + x

    def plane_peer(j, i):
        return (((y + j) % NY) * NZ + z) * NX + (x + i) % NX

    line_steps = [4, 3, 5, 2, 6, 1, 7]
    plane_steps = [(j, i) for j in (2, 1, 3, 0) for i in (2, 1, 3, 0) if i or j]
    sibling = (batch, 1 - tile)

    @pl.when(tile == 0)
    def _():
        pltpu.make_async_copy(first_ref, stage, load_sem).start()

    @pl.when(tile == 1)
    def _():
        pltpu.make_async_copy(second_ref, stage, load_sem).start()

    barrier = pltpu.get_barrier_semaphore()
    greeted = [(line_peer(k), c) for k in line_steps for c in (tile, 1 - tile)]
    greeted += [(plane_peer(j, i), tile) for j, i in plane_steps] + [sibling]
    for device in greeted:
        pl.semaphore_signal(barrier, inc=1, device_id=device, device_id_type=MESH)
    pltpu.make_async_copy(stage, stage, load_sem).wait()
    line[:, z] = stage[pl.ds(z * chunks, chunks)]
    pl.semaphore_wait(barrier, len(greeted))

    def send(phase, source, target, device, arrived=None):
        pltpu.make_async_remote_copy(
            src_ref=source,
            dst_ref=target,
            send_sem=send_sem.at[phase],
            recv_sem=recv_sem.at[phase] if arrived is None else arrived,
            device_id=device,
            device_id_type=MESH,
        ).start()

    def wait(sem, like):
        pltpu.make_async_copy(like, like, sem).wait()

    for k in line_steps:
        source = stage.at[pl.ds((z + k) % NZ * chunks, chunks)]
        send(0, source, line.at[:, z], (line_peer(k), tile), line_sem.at[k])
    for k in [0, 1, 7, 2, 6, 3, 5, 4]:
        origin = (z + NZ - k) % NZ
        piece = line.at[:, origin]
        if k:
            wait(line_sem.at[k], piece)
        for j, i in plane_steps:
            send(1, piece, whole.at[slot, :, origin], (plane_peer(j, i), tile))
    whole[slot] = line[...]
    wait(recv_sem.at[1], whole.at[pl.ds(0, PLANE - 1)])

    inverse = []
    for c in range(chunks):
        values = whole_rows[:, c].reshape(total_rows, LANES).astype(jnp.float32)
        mean = jnp.sum(values, 0, keepdims=True) / total_rows
        centered = values - mean
        variance = jnp.sum(centered * centered, 0, keepdims=True) / total_rows
        inverse.append(lax.rsqrt(variance + epsilon))
        norm[:, :, c * LANES : (c + 1) * LANES] = (
            (centered * inverse[c]).astype(jnp.bfloat16).reshape(PLANE, rows, LANES)
        )
    inverse = jnp.concatenate(inverse, 1)
    width = chunks * LANES
    gram_out[...] = lax.dot_general(
        norm[slot],
        norm[...].reshape(total_rows, width),
        (((1,), (1,)), ((), ())),
        preferred_element_type=jnp.float32,
    ).astype(jnp.bfloat16)

    for k in line_steps:
        send(2, gram_out, gram_in.at[z], (line_peer(k), 1 - tile))
    send(2, gram_out, gram_in.at[z], sibling)
    send(3, norm, other, sibling)
    wait(recv_sem.at[3], other)
    paired = []
    for c in range(chunks):
        lanes = slice(c * LANES, (c + 1) * LANES)
        product = norm[:, :, lanes].astype(jnp.float32) * other[:, :, lanes].astype(jnp.float32)
        paired.append(jnp.sum(product.reshape(total_rows, LANES), 0, keepdims=True))
    paired = jnp.concatenate(paired, 1) / total_rows
    excess = (paired - 1.0) - decorrelation * paired
    mine = norm[slot].astype(jnp.float32)
    direct = excess * other[slot].astype(jnp.float32)
    wait(recv_sem.at[2], gram_in)
    gram = jnp.sum(gram_in[...].astype(jnp.float32), 0) * (decorrelation / total_rows)
    high = gram.astype(jnp.bfloat16)
    low = (gram - high.astype(jnp.float32)).astype(jnp.bfloat16)
    both = jnp.dot(
        jnp.concatenate([high, low], 0),
        norm[...].reshape(total_rows, width),
        preferred_element_type=jnp.float32,
    )
    pull = both[:rows] + both[rows:] + direct
    stat_out[...] = jnp.sum(pull * mine, 0, keepdims=True)

    for j, i in plane_steps:
        send(4, stat_out, stat_in.at[slot], (plane_peer(j, i), tile))
    stat_in[slot] = stat_out[...]
    wait(recv_sem.at[4], stat_in.at[pl.ds(0, PLANE - 1)])
    stat = jnp.sum(stat_in[...], 0) / total_rows
    grad = (inverse * (pull - mine * stat)).astype(jnp.bfloat16)
    for c in range(chunks):
        grad_rows[c] = grad[:, c * LANES : (c + 1) * LANES]

    owner = z // (NZ // CORES)
    target = grads_ref.at[tile, pl.ds(z % (NZ // CORES) * chunks, chunks)]
    for k in line_steps:
        send(5, grad_out.at[:, (z + k) % NZ], target, (line_peer(k), owner))

    @pl.when(owner == tile)
    def _():
        pltpu.make_async_copy(grad_out.at[:, z], target, recv_sem.at[5]).start()

    @pl.when(owner != tile)
    def _():
        send(6, grad_out.at[:, z], target, sibling, recv_sem.at[5])

    wait(recv_sem.at[5], grads_ref)

    wait(send_sem.at[0], line.at[:, pl.ds(0, NZ - 1)])
    wait(send_sem.at[1], whole.at[pl.ds(0, PLANE - 1)])
    wait(send_sem.at[2], gram_in)
    wait(send_sem.at[3], other)
    wait(send_sem.at[4], stat_in.at[pl.ds(0, PLANE - 1)])
    wait(send_sem.at[5], grad_out.at[:, pl.ds(0, NZ - 1)])

    @pl.when(owner != tile)
    def _():
        wait(send_sem.at[6], grad_out.at[:, 0])


def per_device(first_view, second_view):
    row_count, feature_width = first_view.shape
    chunks = feature_width // (NZ * LANES)
    width = chunks * LANES
    rows = row_count * NZ
    total_rows = rows * PLANE
    half = feature_width // CORES
    bf16, f32 = jnp.bfloat16, jnp.float32
    views = [
        view.reshape(row_count, feature_width // LANES, LANES).transpose(1, 0, 2)
        for view in (first_view, second_view)
    ]
    grads = pl.pallas_call(
        kernel,
        out_shape=jax.ShapeDtypeStruct((2, half // LANES, row_count, LANES), bf16),
        in_specs=[pl.BlockSpec(memory_space=pltpu.HBM)] * 2,
        out_specs=pl.BlockSpec(memory_space=pltpu.VMEM),
        scratch_shapes=[
            pltpu.VMEM((feature_width // LANES, row_count, LANES), bf16),
            pltpu.VMEM((chunks, NZ, row_count, LANES), bf16),
            pltpu.VMEM((PLANE, chunks, NZ, row_count, LANES), bf16),
            pltpu.VMEM((PLANE, rows, width), bf16),
            pltpu.VMEM((PLANE, rows, width), bf16),
            pltpu.VMEM((rows, total_rows), bf16),
            pltpu.VMEM((NZ, rows, total_rows), bf16),
            pltpu.VMEM((1, width), f32),
            pltpu.VMEM((PLANE, 1, width), f32),
            pltpu.VMEM((chunks, NZ, row_count, LANES), bf16),
            pltpu.SemaphoreType.DMA,
            pltpu.SemaphoreType.DMA((NZ,)),
            pltpu.SemaphoreType.DMA((7,)),
            pltpu.SemaphoreType.DMA((6,)),
        ],
        compiler_params=pltpu.CompilerParams(
            collective_id=0, has_side_effects=True, vmem_limit_bytes=32 << 20
        ),
        name="twins",
    )(*[pltpu.with_memory_space_constraint(view, pltpu.HBM) for view in views])
    return tuple(grads[v].transpose(1, 0, 2).reshape(row_count, half) for v in range(2))


def solution(mesh):
    return jax.shard_map(
        per_device,
        mesh=mesh,
        in_specs=(P("batch", None), P("batch", None)),
        out_specs=(P("batch", "tile"), P("batch", "tile")),
        check_vma=False,
    )
```

```python
import jax
import jax.numpy as jnp
from jax import lax
from jax.experimental import pallas as pl
from jax.experimental.pallas import tpu as pltpu
from jax.sharding import PartitionSpec as P

epsilon = 1e-05
decorrelation = 0.0051

NY, NZ, NX = 4, 8, 4
PLANE = NY * NX
CORES = 2
LANES = 128
MESH = pl.DeviceIdType.MESH


def kernel(
    first_ref,
    second_ref,
    grads_ref,
    stage,
    line,
    whole,
    norm,
    other,
    gram_out,
    gram_in,
    stat_out,
    stat_in,
    grad_out,
    load_sem,
    line_sem,
    send_sem,
    recv_sem,
):
    batch = lax.axis_index("batch")
    tile = lax.axis_index("tile")
    x = batch % NX
    z = (batch // NX) % NZ
    y = batch // (NX * NZ)
    slot = y * NX + x
    chunks, pair = line.shape[0], line.shape[2]
    rows = NZ * pair
    total_rows = rows * PLANE
    whole_rows = whole.reshape(PLANE, chunks, rows, LANES)
    grad_rows = grad_out.reshape(chunks, rows, LANES)

    def line_peer(k):
        return (y * NZ + (z + k) % NZ) * NX + x

    def plane_peer(j, i):
        return (((y + j) % NY) * NZ + z) * NX + (x + i) % NX

    def block_of(k):
        turned = (k + 1) % NZ
        return (turned + NZ // 2) % NZ

    line_steps = [4, 3, 5, 2, 6, 1, 7]
    plane_steps = [(j, i) for j in (2, 1, 3, 0) for i in (2, 1, 3, 0) if i or j]
    sibling = (batch, 1 - tile)

    @pl.when(tile == 0)
    def _():
        pltpu.make_async_copy(first_ref, stage, load_sem).start()

    @pl.when(tile == 1)
    def _():
        pltpu.make_async_copy(second_ref, stage, load_sem).start()

    barrier = pltpu.get_barrier_semaphore()
    greeted = [(line_peer(k), c) for k in line_steps for c in (tile, 1 - tile)]
    greeted += [(plane_peer(j, i), tile) for j, i in plane_steps] + [sibling]
    for device in greeted:
        pl.semaphore_signal(barrier, inc=1, device_id=device, device_id_type=MESH)
    pltpu.make_async_copy(stage, stage, load_sem).wait()
    line[:, z] = stage[pl.ds(block_of(z) * chunks, chunks)]
    pl.semaphore_wait(barrier, len(greeted))

    def send(phase, source, target, device, arrived=None):
        pltpu.make_async_remote_copy(
            src_ref=source,
            dst_ref=target,
            send_sem=send_sem.at[phase],
            recv_sem=recv_sem.at[phase] if arrived is None else arrived,
            device_id=device,
            device_id_type=MESH,
        ).start()

    def wait(sem, like):
        pltpu.make_async_copy(like, like, sem).wait()

    for k in line_steps:
        source = stage.at[pl.ds(block_of((z + k) % NZ) * chunks, chunks)]
        send(0, source, line.at[:, z], (line_peer(k), tile), line_sem.at[k])
    for k in [0, 1, 7, 2, 6, 3, 5, 4]:
        origin = (z + NZ - k) % NZ
        piece = line.at[:, origin]
        if k:
            wait(line_sem.at[k], piece)
        for j, i in plane_steps:
            send(1, piece, whole.at[slot, :, origin], (plane_peer(j, i), tile))
    whole[slot] = line[...]
    wait(recv_sem.at[1], whole.at[pl.ds(0, PLANE - 1)])

    inverse = []
    for c in range(chunks):
        values = whole_rows[:, c].reshape(total_rows, LANES).astype(jnp.float32)
        mean = jnp.sum(values, 0, keepdims=True) / total_rows
        centered = values - mean
        variance = jnp.sum(centered * centered, 0, keepdims=True) / total_rows
        inverse.append(lax.rsqrt(variance + epsilon))
        norm[:, :, c * LANES : (c + 1) * LANES] = (
            (centered * inverse[c]).astype(jnp.bfloat16).reshape(PLANE, rows, LANES)
        )
    inverse = jnp.concatenate(inverse, 1)
    width = chunks * LANES
    gram_out[...] = lax.dot_general(
        norm[slot],
        norm[...].reshape(total_rows, width),
        (((1,), (1,)), ((), ())),
        preferred_element_type=jnp.float32,
    ).astype(jnp.bfloat16)

    for k in line_steps:
        send(2, gram_out, gram_in.at[z], (line_peer(k), 1 - tile))
    send(2, gram_out, gram_in.at[z], sibling)
    send(3, norm, other, sibling)
    wait(recv_sem.at[3], other)
    paired = []
    for c in range(chunks):
        lanes = slice(c * LANES, (c + 1) * LANES)
        product = norm[:, :, lanes].astype(jnp.float32) * other[:, :, lanes].astype(jnp.float32)
        paired.append(jnp.sum(product.reshape(total_rows, LANES), 0, keepdims=True))
    paired = jnp.concatenate(paired, 1) / total_rows
    excess = (paired - 1.0) - decorrelation * paired
    mine = norm[slot].astype(jnp.float32)
    direct = excess * other[slot].astype(jnp.float32)
    wait(recv_sem.at[2], gram_in)
    gram = jnp.sum(gram_in[...].astype(jnp.float32), 0) * (decorrelation / total_rows)
    high = gram.astype(jnp.bfloat16)
    low = (gram - high.astype(jnp.float32)).astype(jnp.bfloat16)
    both = jnp.dot(
        jnp.concatenate([high, low], 0),
        norm[...].reshape(total_rows, width),
        preferred_element_type=jnp.float32,
    )
    pull = both[:rows] + both[rows:] + direct
    stat_out[...] = jnp.sum(pull * mine, 0, keepdims=True)

    for j, i in plane_steps:
        send(4, stat_out, stat_in.at[slot], (plane_peer(j, i), tile))
    stat_in[slot] = stat_out[...]
    wait(recv_sem.at[4], stat_in.at[pl.ds(0, PLANE - 1)])
    stat = jnp.sum(stat_in[...], 0) / total_rows
    grad = (inverse * (pull - mine * stat)).astype(jnp.bfloat16)
    for c in range(chunks):
        grad_rows[c] = grad[:, c * LANES : (c + 1) * LANES]

    owner = block_of(z) // (NZ // CORES)
    target = grads_ref.at[tile, pl.ds(block_of(z) % (NZ // CORES) * chunks, chunks)]
    for k in line_steps:
        send(5, grad_out.at[:, (z + k) % NZ], target, (line_peer(k), owner))

    @pl.when(owner == tile)
    def _():
        pltpu.make_async_copy(grad_out.at[:, z], target, recv_sem.at[5]).start()

    @pl.when(owner != tile)
    def _():
        send(6, grad_out.at[:, z], target, sibling, recv_sem.at[5])

    wait(recv_sem.at[5], grads_ref)

    wait(send_sem.at[0], line.at[:, pl.ds(0, NZ - 1)])
    wait(send_sem.at[1], whole.at[pl.ds(0, PLANE - 1)])
    wait(send_sem.at[2], gram_in)
    wait(send_sem.at[3], other)
    wait(send_sem.at[4], stat_in.at[pl.ds(0, PLANE - 1)])
    wait(send_sem.at[5], grad_out.at[:, pl.ds(0, NZ - 1)])

    @pl.when(owner != tile)
    def _():
        wait(send_sem.at[6], grad_out.at[:, 0])


def per_device(first_view, second_view):
    row_count, feature_width = first_view.shape
    chunks = feature_width // (NZ * LANES)
    width = chunks * LANES
    rows = row_count * NZ
    total_rows = rows * PLANE
    half = feature_width // CORES
    bf16, f32 = jnp.bfloat16, jnp.float32
    views = [
        view.reshape(row_count, feature_width // LANES, LANES).transpose(1, 0, 2)
        for view in (first_view, second_view)
    ]
    grads = pl.pallas_call(
        kernel,
        out_shape=jax.ShapeDtypeStruct((2, half // LANES, row_count, LANES), bf16),
        in_specs=[pl.BlockSpec(memory_space=pltpu.HBM)] * 2,
        out_specs=pl.BlockSpec(memory_space=pltpu.VMEM),
        scratch_shapes=[
            pltpu.VMEM((feature_width // LANES, row_count, LANES), bf16),
            pltpu.VMEM((chunks, NZ, row_count, LANES), bf16),
            pltpu.VMEM((PLANE, chunks, NZ, row_count, LANES), bf16),
            pltpu.VMEM((PLANE, rows, width), bf16),
            pltpu.VMEM((PLANE, rows, width), bf16),
            pltpu.VMEM((rows, total_rows), bf16),
            pltpu.VMEM((NZ, rows, total_rows), bf16),
            pltpu.VMEM((1, width), f32),
            pltpu.VMEM((PLANE, 1, width), f32),
            pltpu.VMEM((chunks, NZ, row_count, LANES), bf16),
            pltpu.SemaphoreType.DMA,
            pltpu.SemaphoreType.DMA((NZ,)),
            pltpu.SemaphoreType.DMA((7,)),
            pltpu.SemaphoreType.DMA((6,)),
        ],
        compiler_params=pltpu.CompilerParams(
            collective_id=0, has_side_effects=True, vmem_limit_bytes=32 << 20
        ),
        name="twins",
    )(*[pltpu.with_memory_space_constraint(view, pltpu.HBM) for view in views])
    return tuple(grads[v].transpose(1, 0, 2).reshape(row_count, half) for v in range(2))


def solution(mesh):
    return jax.shard_map(
        per_device,
        mesh=mesh,
        in_specs=(P("batch", None), P("batch", None)),
        out_specs=(P("batch", "tile"), P("batch", "tile")),
        check_vma=False,
    )
```

```python
import jax
import jax.numpy as jnp
from jax import lax
from jax.experimental import pallas as pl
from jax.experimental.pallas import tpu as pltpu
from jax.sharding import PartitionSpec as P

epsilon = 1e-05
decorrelation = 0.0051

NY, NZ, NX = 4, 8, 4
PLANE = NY * NX
CORES = 2
LANES = 128
MESH = pl.DeviceIdType.MESH


def fold(values):
    while values.shape[0] > 8:
        half = values.shape[0] // 2
        values = values[:half] + values[half:]
    return jnp.sum(values, 0, keepdims=True)


def kernel(
    first_ref,
    second_ref,
    grads_ref,
    stage,
    line,
    whole,
    norm,
    other,
    gram_out,
    gram_in,
    stat_out,
    stat_in,
    grad_out,
    load_sem,
    line_sem,
    send_sem,
    recv_sem,
):
    batch = lax.axis_index("batch")
    tile = lax.axis_index("tile")
    x = batch % NX
    z = (batch // NX) % NZ
    y = batch // (NX * NZ)
    slot = y * NX + x
    chunks, pair = line.shape[0], line.shape[2]
    rows = NZ * pair
    total_rows = rows * PLANE
    whole_rows = whole.reshape(PLANE, chunks, rows, LANES)
    grad_rows = grad_out.reshape(chunks, rows, LANES)

    def line_peer(k):
        return (y * NZ + (z + k) % NZ) * NX + x

    def plane_peer(j, i):
        return (((y + j) % NY) * NZ + z) * NX + (x + i) % NX

    def block_of(k):
        turned = (k + 1) % NZ
        return (turned + NZ // 2) % NZ

    line_steps = [4, 3, 5, 2, 6, 1, 7]
    plane_steps = [(j, i) for j in (2, 1, 3, 0) for i in (2, 1, 3, 0) if i or j]
    far_steps = [(j, i) for j, i in plane_steps if min(j, NY - j) + min(i, NX - i) > 2]
    near_steps = [step for step in plane_steps if step not in far_steps]
    sibling = (batch, 1 - tile)

    @pl.when(tile == 0)
    def _():
        pltpu.make_async_copy(first_ref, stage, load_sem).start()

    @pl.when(tile == 1)
    def _():
        pltpu.make_async_copy(second_ref, stage, load_sem).start()

    barrier = pltpu.get_barrier_semaphore()
    greeted = [(line_peer(k), c) for k in line_steps for c in (tile, 1 - tile)]
    greeted += [(plane_peer(j, i), tile) for j, i in plane_steps] + [sibling]
    for device in greeted:
        pl.semaphore_signal(barrier, inc=1, device_id=device, device_id_type=MESH)
    pltpu.make_async_copy(stage, stage, load_sem).wait()
    own = stage.at[pl.ds(block_of(z) * chunks, chunks)]
    pltpu.make_async_copy(own, line.at[:, z], line_sem.at[0]).start()
    pl.semaphore_wait(barrier, len(greeted))

    def send(phase, source, target, device, arrived=None):
        pltpu.make_async_remote_copy(
            src_ref=source,
            dst_ref=target,
            send_sem=send_sem.at[phase],
            recv_sem=recv_sem.at[phase] if arrived is None else arrived,
            device_id=device,
            device_id_type=MESH,
        ).start()

    def wait(sem, like):
        pltpu.make_async_copy(like, like, sem).wait()

    for k in line_steps:
        source = stage.at[pl.ds(block_of((z + k) % NZ) * chunks, chunks)]
        send(0, source, line.at[:, z], (line_peer(k), tile), line_sem.at[k])
    @pl.loop(0, NZ)
    def _(n):
        k = jnp.where(n % 2 == 1, (n + 1) // 2, (NZ - n // 2) % NZ)
        origin = (z + NZ - k) % NZ
        piece = line.at[:, origin]
        wait(line_sem.at[k], piece)
        for j, i in plane_steps:
            send(
                1,
                piece,
                whole.at[slot, :, origin],
                (plane_peer(j, i), tile),
                recv_sem.at[6 if (j, i) in far_steps else 1],
            )

    line_rows = line.reshape(chunks, rows, LANES)
    shifts = [
        jnp.sum(line_rows[c].astype(jnp.float32), 0, keepdims=True) / rows for c in range(chunks)
    ]
    sums = [jnp.zeros((8, LANES), jnp.float32)] * chunks
    squares = [jnp.zeros((8, LANES), jnp.float32)] * chunks

    def gather(source, block_rows):
        for c in range(chunks):
            block = block_rows[c]
            norm[source, :, c * LANES : (c + 1) * LANES] = block
            values = block.astype(jnp.float32) - shifts[c]
            sums[c] += values[:8] + values[8:]
            squares[c] += values[:8] * values[:8] + values[8:] * values[8:]

    gather(slot, line_rows)
    for sem, steps in ((1, near_steps), (6, far_steps)):
        wait(recv_sem.at[sem], whole.at[pl.ds(0, len(steps))])
        for j, i in steps:
            source = (y + NY - j) % NY * NX + (x + NX - i) % NX
            gather(source, whole_rows.at[source])
    moves = [jnp.sum(v, 0, keepdims=True) / total_rows for v in sums]
    means = [s + m for s, m in zip(shifts, moves)]
    inverse = [
        lax.rsqrt(jnp.sum(v, 0, keepdims=True) / total_rows - m * m + epsilon)
        for v, m in zip(squares, moves)
    ]
    for c in range(chunks):
        lanes = slice(c * LANES, (c + 1) * LANES)
        values = norm[:, :, lanes].reshape(total_rows, LANES).astype(jnp.float32)
        norm[:, :, lanes] = (
            ((values - means[c]) * inverse[c]).astype(jnp.bfloat16).reshape(PLANE, rows, LANES)
        )
    inverse = jnp.concatenate(inverse, 1)
    width = chunks * LANES
    gram_out[...] = lax.dot_general(
        norm[slot],
        norm[...].reshape(total_rows, width),
        (((1,), (1,)), ((), ())),
        preferred_element_type=jnp.float32,
    ).astype(jnp.bfloat16)

    for k in line_steps:
        send(2, gram_out, gram_in.at[z], (line_peer(k), 1 - tile))
    send(2, gram_out, gram_in.at[z], sibling)
    send(3, norm, other, sibling)
    wait(recv_sem.at[3], other)
    paired = []
    for c in range(chunks):
        lanes = slice(c * LANES, (c + 1) * LANES)
        product = norm[:, :, lanes].astype(jnp.float32) * other[:, :, lanes].astype(jnp.float32)
        paired.append(fold(product.reshape(total_rows, LANES)))
    paired = jnp.concatenate(paired, 1) / total_rows
    excess = (paired - 1.0) - decorrelation * paired
    mine = norm[slot].astype(jnp.float32)
    direct = excess * other[slot].astype(jnp.float32)
    wait(recv_sem.at[2], gram_in)
    gram = jnp.sum(gram_in[...].astype(jnp.float32), 0) * (decorrelation / total_rows)
    high = gram.astype(jnp.bfloat16)
    low = (gram - high.astype(jnp.float32)).astype(jnp.bfloat16)
    both = jnp.dot(
        jnp.concatenate([high, low], 0),
        norm[...].reshape(total_rows, width),
        preferred_element_type=jnp.float32,
    )
    pull = both[:rows] + both[rows:] + direct
    stat_out[...] = fold(pull * mine)

    for j, i in plane_steps:
        send(4, stat_out, stat_in.at[slot], (plane_peer(j, i), tile))
    stat_in[slot] = stat_out[...]
    wait(recv_sem.at[4], stat_in.at[pl.ds(0, PLANE - 1)])
    stat = jnp.sum(stat_in[...], 0) / total_rows
    grad = (inverse * (pull - mine * stat)).astype(jnp.bfloat16)
    for c in range(chunks):
        grad_rows[c] = grad[:, c * LANES : (c + 1) * LANES]

    owner = block_of(z) // (NZ // CORES)
    target = grads_ref.at[tile, pl.ds(block_of(z) % (NZ // CORES) * chunks, chunks)]
    for k in line_steps:
        send(5, grad_out.at[:, (z + k) % NZ], target, (line_peer(k), owner))

    @pl.when(owner == tile)
    def _():
        pltpu.make_async_copy(grad_out.at[:, z], target, recv_sem.at[5]).start()

    @pl.when(owner != tile)
    def _():
        send(6, grad_out.at[:, z], target, sibling, recv_sem.at[5])

    wait(recv_sem.at[5], grads_ref)

    wait(send_sem.at[0], line.at[:, pl.ds(0, NZ - 1)])
    wait(send_sem.at[1], whole.at[pl.ds(0, PLANE - 1)])
    wait(send_sem.at[2], gram_in)
    wait(send_sem.at[3], other)
    wait(send_sem.at[4], stat_in.at[pl.ds(0, PLANE - 1)])
    wait(send_sem.at[5], grad_out.at[:, pl.ds(0, NZ - 1)])

    @pl.when(owner != tile)
    def _():
        wait(send_sem.at[6], grad_out.at[:, 0])


def per_device(first_view, second_view):
    row_count, feature_width = first_view.shape
    chunks = feature_width // (NZ * LANES)
    width = chunks * LANES
    rows = row_count * NZ
    total_rows = rows * PLANE
    half = feature_width // CORES
    bf16, f32 = jnp.bfloat16, jnp.float32
    views = [
        view.reshape(row_count, feature_width // LANES, LANES).transpose(1, 0, 2)
        for view in (first_view, second_view)
    ]
    grads = pl.pallas_call(
        kernel,
        out_shape=jax.ShapeDtypeStruct((2, half // LANES, row_count, LANES), bf16),
        in_specs=[pl.BlockSpec(memory_space=pltpu.HBM)] * 2,
        out_specs=pl.BlockSpec(memory_space=pltpu.VMEM),
        scratch_shapes=[
            pltpu.VMEM((feature_width // LANES, row_count, LANES), bf16),
            pltpu.VMEM((chunks, NZ, row_count, LANES), bf16),
            pltpu.VMEM((PLANE, chunks, NZ, row_count, LANES), bf16),
            pltpu.VMEM((PLANE, rows, width), bf16),
            pltpu.VMEM((PLANE, rows, width), bf16),
            pltpu.VMEM((rows, total_rows), bf16),
            pltpu.VMEM((NZ, rows, total_rows), bf16),
            pltpu.VMEM((1, width), f32),
            pltpu.VMEM((PLANE, 1, width), f32),
            pltpu.VMEM((chunks, NZ, row_count, LANES), bf16),
            pltpu.SemaphoreType.DMA,
            pltpu.SemaphoreType.DMA((NZ,)),
            pltpu.SemaphoreType.DMA((7,)),
            pltpu.SemaphoreType.DMA((7,)),
        ],
        compiler_params=pltpu.CompilerParams(
            collective_id=0, has_side_effects=True, vmem_limit_bytes=32 << 20
        ),
        name="twins",
    )(*[pltpu.with_memory_space_constraint(view, pltpu.HBM) for view in views])
    return tuple(grads[v].transpose(1, 0, 2).reshape(row_count, half) for v in range(2))


def solution(mesh):
    return jax.shard_map(
        per_device,
        mesh=mesh,
        in_specs=(P("batch", None), P("batch", None)),
        out_specs=(P("batch", "tile"), P("batch", "tile")),
        check_vma=False,
    )
```

```python
import jax
import jax.numpy as jnp
from jax import lax
from jax.experimental import pallas as pl
from jax.experimental.pallas import tpu as pltpu
from jax.sharding import PartitionSpec as P

epsilon = 1e-05
decorrelation = 0.0051

NY, NZ, NX = 4, 8, 4
PLANE = NY * NX
CORES = 2
LANES = 128
MESH = pl.DeviceIdType.MESH


def fold(values):
    while values.shape[0] > 8:
        half = values.shape[0] // 2
        values = values[:half] + values[half:]
    return jnp.sum(values, 0, keepdims=True)


def kernel(
    first_ref,
    second_ref,
    grads_ref,
    stage,
    line,
    whole,
    norm,
    other,
    gram_out,
    gram_in,
    stat_out,
    stat_in,
    grad_out,
    load_sem,
    line_sem,
    send_sem,
    recv_sem,
):
    batch = lax.axis_index("batch")
    tile = lax.axis_index("tile")
    x = batch % NX
    z = (batch // NX) % NZ
    y = batch // (NX * NZ)
    slot = y * NX + x
    chunks, pair = line.shape[0], line.shape[2]
    rows = NZ * pair
    total_rows = rows * PLANE
    whole_rows = whole.reshape(PLANE, chunks, rows, LANES)
    grad_rows = grad_out.reshape(chunks, rows, LANES)

    def line_peer(k):
        return (y * NZ + (z + k) % NZ) * NX + x

    def plane_peer(j, i):
        return (((y + j) % NY) * NZ + z) * NX + (x + i) % NX

    def block_of(k):
        turned = (k + 1) % NZ
        return (turned + NZ // 2) % NZ

    line_steps = [4, 3, 5, 2, 6, 1, 7]
    plane_steps = [(j, i) for j in (2, 1, 3, 0) for i in (2, 1, 3, 0) if i or j]
    far_steps = [(j, i) for j, i in plane_steps if min(j, NY - j) + min(i, NX - i) > 2]
    near_steps = [step for step in plane_steps if step not in far_steps]
    sibling = (batch, 1 - tile)

    @pl.when(tile == 0)
    def _():
        pltpu.make_async_copy(first_ref, stage, load_sem).start()

    @pl.when(tile == 1)
    def _():
        pltpu.make_async_copy(second_ref, stage, load_sem).start()

    barrier = pltpu.get_barrier_semaphore()
    greeted = [(line_peer(k), c) for k in line_steps for c in (tile, 1 - tile)]
    greeted += [(plane_peer(j, i), tile) for j, i in plane_steps] + [sibling]
    for device in greeted:
        pl.semaphore_signal(barrier, inc=1, device_id=device, device_id_type=MESH)
    pltpu.make_async_copy(stage, stage, load_sem).wait()
    own = stage.at[pl.ds(block_of(z) * chunks, chunks)]
    pltpu.make_async_copy(own, line.at[:, z], line_sem.at[0]).start()
    pl.semaphore_wait(barrier, len(greeted))

    def send(phase, source, target, device, arrived=None):
        pltpu.make_async_remote_copy(
            src_ref=source,
            dst_ref=target,
            send_sem=send_sem.at[phase],
            recv_sem=recv_sem.at[phase] if arrived is None else arrived,
            device_id=device,
            device_id_type=MESH,
        ).start()

    def wait(sem, like):
        pltpu.make_async_copy(like, like, sem).wait()

    for k in line_steps:
        source = stage.at[pl.ds(block_of((z + k) % NZ) * chunks, chunks)]
        send(0, source, line.at[:, z], (line_peer(k), tile), line_sem.at[k])
    @pl.loop(0, NZ)
    def _(n):
        k = jnp.where(n % 2 == 1, (n + 1) // 2, (NZ - n // 2) % NZ)
        origin = (z + NZ - k) % NZ
        piece = line.at[:, origin]
        wait(line_sem.at[k], piece)
        for j, i in plane_steps:
            send(
                1,
                piece,
                whole.at[slot, :, origin],
                (plane_peer(j, i), tile),
                recv_sem.at[6 if (j, i) in far_steps else 1],
            )

    line_rows = line.reshape(chunks, rows, LANES)
    shifts = [
        jnp.sum(line_rows[c].astype(jnp.float32), 0, keepdims=True) / rows for c in range(chunks)
    ]
    sums = [jnp.zeros((8, LANES), jnp.float32)] * chunks
    squares = [jnp.zeros((8, LANES), jnp.float32)] * chunks

    def gather(source, block_rows):
        for c in range(chunks):
            block = block_rows[c]
            norm[source, :, c * LANES : (c + 1) * LANES] = block
            values = block.astype(jnp.float32) - shifts[c]
            sums[c] += values[:8] + values[8:]
            squares[c] += values[:8] * values[:8] + values[8:] * values[8:]

    gather(slot, line_rows)
    for sem, steps in ((1, near_steps), (6, far_steps)):
        wait(recv_sem.at[sem], whole.at[pl.ds(0, len(steps))])
        for j, i in steps:
            source = (y + NY - j) % NY * NX + (x + NX - i) % NX
            gather(source, whole_rows.at[source])
    moves = [jnp.sum(v, 0, keepdims=True) / total_rows for v in sums]
    means = [s + m for s, m in zip(shifts, moves)]
    inverse = [
        lax.rsqrt(jnp.sum(v, 0, keepdims=True) / total_rows - m * m + epsilon)
        for v, m in zip(squares, moves)
    ]
    def normalized(values, c):
        return ((values.astype(jnp.float32) - means[c]) * inverse[c]).astype(jnp.bfloat16)

    width = chunks * LANES
    gram, mine = jnp.zeros((rows, total_rows), jnp.float32), []
    for c in range(0, chunks, 2):
        pair_rows = []
        for d in (c, c + 1):
            lanes = slice(d * LANES, (d + 1) * LANES)
            values = normalized(norm[:, :, lanes].reshape(total_rows, LANES), d)
            norm[:, :, lanes] = values.reshape(PLANE, rows, LANES)
            pair_rows.append(values)
            mine.append(normalized(line_rows[d], d))
        gram += lax.dot_general(
            jnp.concatenate(mine[-2:], 1),
            jnp.concatenate(pair_rows, 1),
            (((1,), (1,)), ((), ())),
            preferred_element_type=jnp.float32,
        )
    inverse = jnp.concatenate(inverse, 1)
    mine = jnp.concatenate(mine, 1).astype(jnp.float32)
    gram_out[...] = gram.astype(jnp.bfloat16)

    for k in line_steps:
        send(2, gram_out, gram_in.at[z], (line_peer(k), 1 - tile))
    send(2, gram_out, gram_in.at[z], sibling)
    send(3, norm, other, sibling)
    wait(recv_sem.at[3], other)
    paired = []
    for c in range(chunks):
        lanes = slice(c * LANES, (c + 1) * LANES)
        product = norm[:, :, lanes].astype(jnp.float32) * other[:, :, lanes].astype(jnp.float32)
        paired.append(fold(product.reshape(total_rows, LANES)))
    paired = jnp.concatenate(paired, 1) / total_rows
    excess = (paired - 1.0) - decorrelation * paired
    direct = excess * other[slot].astype(jnp.float32)
    wait(recv_sem.at[2], gram_in)
    gram = jnp.sum(gram_in[...].astype(jnp.float32), 0) * (decorrelation / total_rows)
    high = gram.astype(jnp.bfloat16)
    low = (gram - high.astype(jnp.float32)).astype(jnp.bfloat16)
    both = jnp.dot(
        jnp.concatenate([high, low], 0),
        norm[...].reshape(total_rows, width),
        preferred_element_type=jnp.float32,
    )
    pull = both[:rows] + both[rows:] + direct
    stat = fold(pull * mine)
    for c in range(chunks):
        stat_out[c : c + 1] = stat[:, c * LANES : (c + 1) * LANES]

    for j, i in plane_steps:
        send(4, stat_out, stat_in.at[slot], (plane_peer(j, i), tile))
    stat_in[slot] = stat_out[...]
    wait(recv_sem.at[4], stat_in.at[pl.ds(0, PLANE - 1)])
    stat = jnp.sum(stat_in[...], 0) / total_rows
    for c in range(chunks):
        lanes = slice(c * LANES, (c + 1) * LANES)
        grad = inverse[:, lanes] * (pull[:, lanes] - mine[:, lanes] * stat[c : c + 1])
        grad_rows[c] = grad.astype(jnp.bfloat16)

    owner = block_of(z) // (NZ // CORES)
    target = grads_ref.at[tile, pl.ds(block_of(z) % (NZ // CORES) * chunks, chunks)]
    for k in line_steps:
        send(5, grad_out.at[:, (z + k) % NZ], target, (line_peer(k), owner))

    @pl.when(owner == tile)
    def _():
        pltpu.make_async_copy(grad_out.at[:, z], target, recv_sem.at[5]).start()

    @pl.when(owner != tile)
    def _():
        send(6, grad_out.at[:, z], target, sibling, recv_sem.at[5])

    wait(recv_sem.at[5], grads_ref)

    wait(send_sem.at[0], line.at[:, pl.ds(0, NZ - 1)])
    wait(send_sem.at[1], whole.at[pl.ds(0, PLANE - 1)])
    wait(send_sem.at[2], gram_in)
    wait(send_sem.at[3], other)
    wait(send_sem.at[4], stat_in.at[pl.ds(0, PLANE - 1)])
    wait(send_sem.at[5], grad_out.at[:, pl.ds(0, NZ - 1)])

    @pl.when(owner != tile)
    def _():
        wait(send_sem.at[6], grad_out.at[:, 0])


def per_device(first_view, second_view):
    row_count, feature_width = first_view.shape
    chunks = feature_width // (NZ * LANES)
    width = chunks * LANES
    rows = row_count * NZ
    total_rows = rows * PLANE
    half = feature_width // CORES
    bf16, f32 = jnp.bfloat16, jnp.float32
    views = [
        view.reshape(row_count, feature_width // LANES, LANES).transpose(1, 0, 2)
        for view in (first_view, second_view)
    ]
    grads = pl.pallas_call(
        kernel,
        out_shape=jax.ShapeDtypeStruct((2, half // LANES, row_count, LANES), bf16),
        in_specs=[pl.BlockSpec(memory_space=pltpu.HBM)] * 2,
        out_specs=pl.BlockSpec(memory_space=pltpu.VMEM),
        scratch_shapes=[
            pltpu.VMEM((feature_width // LANES, row_count, LANES), bf16),
            pltpu.VMEM((chunks, NZ, row_count, LANES), bf16),
            pltpu.VMEM((PLANE, chunks, NZ, row_count, LANES), bf16),
            pltpu.VMEM((PLANE, rows, width), bf16),
            pltpu.VMEM((PLANE, rows, width), bf16),
            pltpu.VMEM((rows, total_rows), bf16),
            pltpu.VMEM((NZ, rows, total_rows), bf16),
            pltpu.VMEM((chunks, LANES), f32),
            pltpu.VMEM((PLANE, chunks, LANES), f32),
            pltpu.VMEM((chunks, NZ, row_count, LANES), bf16),
            pltpu.SemaphoreType.DMA,
            pltpu.SemaphoreType.DMA((NZ,)),
            pltpu.SemaphoreType.DMA((7,)),
            pltpu.SemaphoreType.DMA((7,)),
        ],
        compiler_params=pltpu.CompilerParams(
            collective_id=0, has_side_effects=True, vmem_limit_bytes=32 << 20
        ),
        name="twins",
    )(*[pltpu.with_memory_space_constraint(view, pltpu.HBM) for view in views])
    return tuple(grads[v].transpose(1, 0, 2).reshape(row_count, half) for v in range(2))


def solution(mesh):
    return jax.shard_map(
        per_device,
        mesh=mesh,
        in_specs=(P("batch", None), P("batch", None)),
        out_specs=(P("batch", "tile"), P("batch", "tile")),
        check_vma=False,
    )
```

```python
import jax
import jax.numpy as jnp
from jax import lax
from jax.experimental import pallas as pl
from jax.experimental.pallas import tpu as pltpu
from jax.sharding import PartitionSpec as P

epsilon = 1e-05
decorrelation = 0.0051

NY, NZ, NX = 4, 8, 4
PLANE = NY * NX
CORES = 2
LANES = 128
MESH = pl.DeviceIdType.MESH


def fold(values):
    while values.shape[0] > 8:
        half = values.shape[0] // 2
        values = values[:half] + values[half:]
    return jnp.sum(values, 0, keepdims=True)


def kernel(
    first_ref,
    second_ref,
    grads_ref,
    stage,
    line,
    whole,
    norm,
    other,
    gram_out,
    gram_in,
    stat_out,
    stat_in,
    grad_out,
    load_sem,
    line_sem,
    send_sem,
    recv_sem,
):
    batch = lax.axis_index("batch")
    tile = lax.axis_index("tile")
    x = batch % NX
    z = (batch // NX) % NZ
    y = batch // (NX * NZ)
    slot = y * NX + x
    chunks, pair = line.shape[0], line.shape[2]
    rows = NZ * pair
    total_rows = rows * PLANE
    whole_rows = whole.reshape(PLANE, chunks, rows, LANES)
    grad_rows = grad_out.reshape(chunks, rows, LANES)

    def line_peer(k):
        return (y * NZ + (z + k) % NZ) * NX + x

    def plane_peer(j, i):
        return (((y + j) % NY) * NZ + z) * NX + (x + i) % NX

    def block_of(k):
        turned = (k + 1) % NZ
        return (turned + NZ // 2) % NZ

    line_steps = [4, 3, 5, 2, 6, 1, 7]
    plane_steps = [(j, i) for j in (2, 1, 3, 0) for i in (2, 1, 3, 0) if i or j]
    far_steps = [(j, i) for j, i in plane_steps if min(j, NY - j) + min(i, NX - i) > 2]
    near_steps = [step for step in plane_steps if step not in far_steps]
    sibling = (batch, 1 - tile)

    barrier = pltpu.get_barrier_semaphore()
    greeted = [(line_peer(k), tile) for k in line_steps]
    greeted += [(plane_peer(j, i), tile) for j, i in plane_steps] + [sibling]
    for device in greeted:
        pl.semaphore_signal(barrier, inc=1, device_id=device, device_id_type=MESH)
    @pl.when(tile == 0)
    def _():
        pltpu.make_async_copy(first_ref, stage, load_sem).start()

    @pl.when(tile == 1)
    def _():
        pltpu.make_async_copy(second_ref, stage, load_sem).start()

    pltpu.make_async_copy(stage, stage, load_sem).wait()
    own = stage.at[pl.ds(block_of(z) * chunks, chunks)]
    pltpu.make_async_copy(own, line.at[:, z], line_sem.at[0]).start()
    pl.semaphore_wait(barrier, len(greeted))

    def send(phase, source, target, device, arrived=None):
        pltpu.make_async_remote_copy(
            src_ref=source,
            dst_ref=target,
            send_sem=send_sem.at[phase],
            recv_sem=recv_sem.at[phase] if arrived is None else arrived,
            device_id=device,
            device_id_type=MESH,
        ).start()

    def wait(sem, like):
        pltpu.make_async_copy(like, like, sem).wait()

    for k in line_steps:
        source = stage.at[pl.ds(block_of((z + k) % NZ) * chunks, chunks)]
        send(0, source, line.at[:, z], (line_peer(k), tile), line_sem.at[k])
    @pl.loop(0, NZ)
    def _(n):
        k = jnp.where(n % 2 == 1, (n + 1) // 2, (NZ - n // 2) % NZ)
        origin = (z + NZ - k) % NZ
        piece = line.at[:, origin]
        wait(line_sem.at[k], piece)
        for j, i in plane_steps:
            send(
                1,
                piece,
                whole.at[slot, :, origin],
                (plane_peer(j, i), tile),
                recv_sem.at[6 if (j, i) in far_steps else 1],
            )

    line_rows = line.reshape(chunks, rows, LANES)
    shifts = [
        jnp.sum(line_rows[c].astype(jnp.float32), 0, keepdims=True) / rows for c in range(chunks)
    ]
    sums = [jnp.zeros((8, LANES), jnp.float32)] * chunks
    squares = [jnp.zeros((8, LANES), jnp.float32)] * chunks

    def gather(source, block_rows):
        for c in range(chunks):
            block = block_rows[c]
            norm[source, :, c * LANES : (c + 1) * LANES] = block
            values = block.astype(jnp.float32) - shifts[c]
            sums[c] += values[:8] + values[8:]
            squares[c] += values[:8] * values[:8] + values[8:] * values[8:]

    gather(slot, line_rows)
    for sem, steps in ((1, near_steps), (6, far_steps)):
        wait(recv_sem.at[sem], whole.at[pl.ds(0, len(steps))])
        for j, i in steps:
            source = (y + NY - j) % NY * NX + (x + NX - i) % NX
            gather(source, whole_rows.at[source])
    moves = [jnp.sum(v, 0, keepdims=True) / total_rows for v in sums]
    means = [s + m for s, m in zip(shifts, moves)]
    inverse = [
        lax.rsqrt(jnp.sum(v, 0, keepdims=True) / total_rows - m * m + epsilon)
        for v, m in zip(squares, moves)
    ]
    def normalized(values, c):
        return ((values.astype(jnp.float32) - means[c]) * inverse[c]).astype(jnp.bfloat16)

    width = chunks * LANES
    gram, mine = jnp.zeros((rows, total_rows), jnp.float32), []
    for c in range(0, chunks, 2):
        pair_rows = []
        for d in (c, c + 1):
            lanes = slice(d * LANES, (d + 1) * LANES)
            values = normalized(norm[:, :, lanes].reshape(total_rows, LANES), d)
            norm[:, :, lanes] = values.reshape(PLANE, rows, LANES)
            pair_rows.append(values)
            mine.append(normalized(line_rows[d], d))
        gram += lax.dot_general(
            jnp.concatenate(mine[-2:], 1),
            jnp.concatenate(pair_rows, 1),
            (((1,), (1,)), ((), ())),
            preferred_element_type=jnp.float32,
        )
    inverse = jnp.concatenate(inverse, 1)
    mine = jnp.concatenate(mine, 1).astype(jnp.float32)
    gram_out[...] = gram.astype(jnp.bfloat16)

    for k in line_steps:
        send(2, gram_out, gram_in.at[z], (line_peer(k), 1 - tile))
    send(2, gram_out, gram_in.at[z], sibling)
    send(3, norm, other, sibling)
    wait(recv_sem.at[3], other)
    paired = []
    for c in range(chunks):
        lanes = slice(c * LANES, (c + 1) * LANES)
        product = norm[:, :, lanes].astype(jnp.float32) * other[:, :, lanes].astype(jnp.float32)
        paired.append(fold(product.reshape(total_rows, LANES)))
    paired = jnp.concatenate(paired, 1) / total_rows
    excess = (paired - 1.0) - decorrelation * paired
    direct = excess * other[slot].astype(jnp.float32)
    wait(recv_sem.at[2], gram_in)
    gram = jnp.sum(gram_in[...].astype(jnp.float32), 0) * (decorrelation / total_rows)
    high = gram.astype(jnp.bfloat16)
    low = (gram - high.astype(jnp.float32)).astype(jnp.bfloat16)
    both = jnp.dot(
        jnp.concatenate([high, low], 0),
        norm[...].reshape(total_rows, width),
        preferred_element_type=jnp.float32,
    )
    pull = both[:rows] + both[rows:] + direct
    stat = fold(pull * mine)
    for c in range(chunks):
        stat_out[c : c + 1] = stat[:, c * LANES : (c + 1) * LANES]

    for j, i in plane_steps:
        send(4, stat_out, stat_in.at[slot], (plane_peer(j, i), tile))
    stat_in[slot] = stat_out[...]
    wait(recv_sem.at[4], stat_in.at[pl.ds(0, PLANE - 1)])
    stat = jnp.sum(stat_in[...], 0) / total_rows
    for c in range(chunks):
        lanes = slice(c * LANES, (c + 1) * LANES)
        grad = inverse[:, lanes] * (pull[:, lanes] - mine[:, lanes] * stat[c : c + 1])
        grad_rows[c] = grad.astype(jnp.bfloat16)

    owner = block_of(z) // (NZ // CORES)
    target = grads_ref.at[tile, pl.ds(block_of(z) % (NZ // CORES) * chunks, chunks)]
    for k in line_steps:
        send(5, grad_out.at[:, (z + k) % NZ], target, (line_peer(k), owner))

    @pl.when(owner == tile)
    def _():
        pltpu.make_async_copy(grad_out.at[:, z], target, recv_sem.at[5]).start()

    @pl.when(owner != tile)
    def _():
        send(6, grad_out.at[:, z], target, sibling, recv_sem.at[5])

    wait(recv_sem.at[5], grads_ref)

    wait(send_sem.at[0], line.at[:, pl.ds(0, NZ - 1)])
    wait(send_sem.at[1], whole.at[pl.ds(0, PLANE - 1)])
    wait(send_sem.at[2], gram_in)
    wait(send_sem.at[3], other)
    wait(send_sem.at[4], stat_in.at[pl.ds(0, PLANE - 1)])
    wait(send_sem.at[5], grad_out.at[:, pl.ds(0, NZ - 1)])

    @pl.when(owner != tile)
    def _():
        wait(send_sem.at[6], grad_out.at[:, 0])


def per_device(first_view, second_view):
    row_count, feature_width = first_view.shape
    chunks = feature_width // (NZ * LANES)
    width = chunks * LANES
    rows = row_count * NZ
    total_rows = rows * PLANE
    half = feature_width // CORES
    bf16, f32 = jnp.bfloat16, jnp.float32
    views = [
        view.reshape(row_count, feature_width // LANES, LANES).transpose(1, 0, 2)
        for view in (first_view, second_view)
    ]
    grads = pl.pallas_call(
        kernel,
        out_shape=jax.ShapeDtypeStruct((2, half // LANES, row_count, LANES), bf16),
        in_specs=[pl.BlockSpec(memory_space=pltpu.HBM)] * 2,
        out_specs=pl.BlockSpec(memory_space=pltpu.VMEM),
        scratch_shapes=[
            pltpu.VMEM((feature_width // LANES, row_count, LANES), bf16),
            pltpu.VMEM((chunks, NZ, row_count, LANES), bf16),
            pltpu.VMEM((PLANE, chunks, NZ, row_count, LANES), bf16),
            pltpu.VMEM((PLANE, rows, width), bf16),
            pltpu.VMEM((PLANE, rows, width), bf16),
            pltpu.VMEM((rows, total_rows), bf16),
            pltpu.VMEM((NZ, rows, total_rows), bf16),
            pltpu.VMEM((chunks, LANES), f32),
            pltpu.VMEM((PLANE, chunks, LANES), f32),
            pltpu.VMEM((chunks, NZ, row_count, LANES), bf16),
            pltpu.SemaphoreType.DMA,
            pltpu.SemaphoreType.DMA((NZ,)),
            pltpu.SemaphoreType.DMA((7,)),
            pltpu.SemaphoreType.DMA((7,)),
        ],
        compiler_params=pltpu.CompilerParams(
            collective_id=0, has_side_effects=True, vmem_limit_bytes=32 << 20
        ),
        name="twins",
    )(*[pltpu.with_memory_space_constraint(view, pltpu.HBM) for view in views])
    return tuple(grads[v].transpose(1, 0, 2).reshape(row_count, half) for v in range(2))


def solution(mesh):
    return jax.shard_map(
        per_device,
        mesh=mesh,
        in_specs=(P("batch", None), P("batch", None)),
        out_specs=(P("batch", "tile"), P("batch", "tile")),
        check_vma=False,
    )
```

```python
import jax
import jax.numpy as jnp
from jax import lax
from jax.experimental import pallas as pl
from jax.experimental.pallas import tpu as pltpu
from jax.sharding import PartitionSpec as P

epsilon = 1e-05
decorrelation = 0.0051

NY, NZ, NX = 4, 8, 4
PLANE = NY * NX
CORES = 2
LANES = 128
MESH = pl.DeviceIdType.MESH


def fold(values):
    while values.shape[0] > 8:
        half = values.shape[0] // 2
        values = values[:half] + values[half:]
    return jnp.sum(values, 0, keepdims=True)


def kernel(
    first_ref,
    second_ref,
    grads_ref,
    stage,
    line,
    whole,
    norm,
    other,
    gram_out,
    gram_in,
    stat_out,
    stat_in,
    grad_out,
    load_sem,
    line_sem,
    send_sem,
    recv_sem,
):
    batch = lax.axis_index("batch")
    tile = lax.axis_index("tile")
    x = batch % NX
    z = (batch // NX) % NZ
    y = batch // (NX * NZ)
    slot = y * NX + x
    chunks, pair = line.shape[0], line.shape[2]
    rows = NZ * pair
    total_rows = rows * PLANE
    whole_rows = whole.reshape(PLANE, chunks, rows, LANES)
    grad_rows = grad_out.reshape(chunks, rows, LANES)

    def line_peer(k):
        return (y * NZ + (z + k) % NZ) * NX + x

    def plane_peer(j, i):
        return (((y + j) % NY) * NZ + z) * NX + (x + i) % NX

    def block_of(k):
        turned = (k + 1) % NZ
        return (turned + NZ // 2) % NZ

    line_steps = [4, 3, 5, 2, 6, 1, 7]
    plane_steps = [(j, i) for j in (2, 1, 3, 0) for i in (2, 1, 3, 0) if i or j]
    far_steps = [(j, i) for j, i in plane_steps if min(j, NY - j) + min(i, NX - i) > 2]
    near_steps = [step for step in plane_steps if step not in far_steps]
    sibling = (batch, 1 - tile)

    @pl.when(tile == 0)
    def _():
        pltpu.make_async_copy(first_ref, stage, load_sem).start()

    @pl.when(tile == 1)
    def _():
        pltpu.make_async_copy(second_ref, stage, load_sem).start()

    barrier = pltpu.get_barrier_semaphore()
    greeted = [(line_peer(k), c) for k in line_steps for c in (tile, 1 - tile)]
    greeted += [(plane_peer(j, i), tile) for j, i in plane_steps] + [sibling]
    for device in greeted:
        pl.semaphore_signal(barrier, inc=1, device_id=device, device_id_type=MESH)
    pltpu.make_async_copy(stage, stage, load_sem).wait()
    own = stage.at[pl.ds(block_of(z) * chunks, chunks)]
    pltpu.make_async_copy(own, line.at[:, z], line_sem.at[0]).start()
    pl.semaphore_wait(barrier, len(greeted))

    def send(phase, source, target, device, arrived=None):
        pltpu.make_async_remote_copy(
            src_ref=source,
            dst_ref=target,
            send_sem=send_sem.at[phase],
            recv_sem=recv_sem.at[phase] if arrived is None else arrived,
            device_id=device,
            device_id_type=MESH,
        ).start()

    def wait(sem, like):
        pltpu.make_async_copy(like, like, sem).wait()

    for k in line_steps:
        source = stage.at[pl.ds(block_of((z + k) % NZ) * chunks, chunks)]
        send(0, source, line.at[:, z], (line_peer(k), tile), line_sem.at[k])
    @pl.loop(0, NZ)
    def _(n):
        k = jnp.where(n % 2 == 1, (n + 1) // 2, (NZ - n // 2) % NZ)
        origin = (z + NZ - k) % NZ
        piece = line.at[:, origin]
        wait(line_sem.at[k], piece)
        for j, i in plane_steps:
            send(
                1,
                piece,
                whole.at[slot, :, origin],
                (plane_peer(j, i), tile),
                recv_sem.at[6 if (j, i) in far_steps else 1],
            )

    line_rows = line.reshape(chunks, rows, LANES)
    shifts = [
        jnp.sum(line_rows[c].astype(jnp.float32), 0, keepdims=True) / rows for c in range(chunks)
    ]
    sums = [jnp.zeros((8, LANES), jnp.float32)] * chunks
    squares = [jnp.zeros((8, LANES), jnp.float32)] * chunks

    def gather(source, block_rows):
        for c in range(chunks):
            block = block_rows[c]
            norm[source, :, c * LANES : (c + 1) * LANES] = block
            values = block.astype(jnp.float32) - shifts[c]
            sums[c] += values[:8] + values[8:]
            squares[c] += values[:8] * values[:8] + values[8:] * values[8:]

    gather(slot, line_rows)
    for sem, steps in ((1, near_steps), (6, far_steps)):
        wait(recv_sem.at[sem], whole.at[pl.ds(0, len(steps))])
        for j, i in steps:
            source = (y + NY - j) % NY * NX + (x + NX - i) % NX
            gather(source, whole_rows.at[source])
    moves = [jnp.sum(v, 0, keepdims=True) / total_rows for v in sums]
    means = [s + m for s, m in zip(shifts, moves)]
    inverse = [
        lax.rsqrt(jnp.sum(v, 0, keepdims=True) / total_rows - m * m + epsilon)
        for v, m in zip(squares, moves)
    ]
    def normalized(values, c):
        return ((values.astype(jnp.float32) - means[c]) * inverse[c]).astype(jnp.bfloat16)

    width = chunks * LANES
    gram, mine = jnp.zeros((rows, total_rows), jnp.float32), []
    for c in range(0, chunks, 2):
        pair_rows = []
        for d in (c, c + 1):
            lanes = slice(d * LANES, (d + 1) * LANES)
            values = normalized(norm[:, :, lanes].reshape(total_rows, LANES), d)
            norm[:, :, lanes] = values.reshape(PLANE, rows, LANES)
            pair_rows.append(values)
            mine.append(normalized(line_rows[d], d))
        gram += lax.dot_general(
            jnp.concatenate(mine[-2:], 1),
            jnp.concatenate(pair_rows, 1),
            (((1,), (1,)), ((), ())),
            preferred_element_type=jnp.float32,
        )
    inverse = jnp.concatenate(inverse, 1)
    mine = jnp.concatenate(mine, 1).astype(jnp.float32)
    gram_out[...] = gram.astype(jnp.bfloat16)

    for k in line_steps:
        send(2, gram_out, gram_in.at[z], (line_peer(k), 1 - tile))
    send(2, gram_out, gram_in.at[z], sibling)
    send(3, norm, other, sibling)
    wait(recv_sem.at[3], other)
    paired = []
    for c in range(chunks):
        lanes = slice(c * LANES, (c + 1) * LANES)
        product = norm[:, :, lanes].astype(jnp.float32) * other[:, :, lanes].astype(jnp.float32)
        paired.append(fold(product.reshape(total_rows, LANES)))
    paired = jnp.concatenate(paired, 1) / total_rows
    excess = (paired - 1.0) - decorrelation * paired
    direct = excess * other[slot].astype(jnp.float32)
    wait(recv_sem.at[2], gram_in)
    gram = jnp.sum(gram_in[...].astype(jnp.float32), 0) * (decorrelation / total_rows)
    high = gram.astype(jnp.bfloat16)
    low = (gram - high.astype(jnp.float32)).astype(jnp.bfloat16)
    both = jnp.dot(
        jnp.concatenate([high, low], 0),
        norm[...].reshape(total_rows, width),
        preferred_element_type=jnp.float32,
    )
    pull = both[:rows] + both[rows:] + direct
    stat = fold(pull * mine)
    for c in range(chunks):
        stat_out[c : c + 1] = stat[:, c * LANES : (c + 1) * LANES]

    for j, i in plane_steps:
        arrived = recv_sem.at[5 if (j, i) in far_steps else 4]
        send(4, stat_out, stat_in.at[slot], (plane_peer(j, i), tile), arrived)
    scaled_pull, scaled_mine = inverse * pull, inverse * mine
    stat = stat_out[...]
    for sem, steps in ((4, near_steps), (5, far_steps)):
        wait(recv_sem.at[sem], stat_in.at[pl.ds(0, len(steps))])
        for j, i in steps:
            stat += stat_in[(y + NY - j) % NY * NX + (x + NX - i) % NX]
    stat = stat / total_rows
    for c in range(chunks):
        lanes = slice(c * LANES, (c + 1) * LANES)
        grad = scaled_pull[:, lanes] - scaled_mine[:, lanes] * stat[c : c + 1]
        grad_rows[c] = grad.astype(jnp.bfloat16)

    owner = block_of(z) // (NZ // CORES)
    target = grads_ref.at[tile, pl.ds(block_of(z) % (NZ // CORES) * chunks, chunks)]
    for k in line_steps:
        send(5, grad_out.at[:, (z + k) % NZ], target, (line_peer(k), owner), recv_sem.at[7])

    @pl.when(owner == tile)
    def _():
        pltpu.make_async_copy(grad_out.at[:, z], target, recv_sem.at[7]).start()

    @pl.when(owner != tile)
    def _():
        send(6, grad_out.at[:, z], target, sibling, recv_sem.at[7])

    wait(recv_sem.at[7], grads_ref)

    wait(send_sem.at[0], line.at[:, pl.ds(0, NZ - 1)])
    wait(send_sem.at[1], whole.at[pl.ds(0, PLANE - 1)])
    wait(send_sem.at[2], gram_in)
    wait(send_sem.at[3], other)
    wait(send_sem.at[4], stat_in.at[pl.ds(0, PLANE - 1)])
    wait(send_sem.at[5], grad_out.at[:, pl.ds(0, NZ - 1)])

    @pl.when(owner != tile)
    def _():
        wait(send_sem.at[6], grad_out.at[:, 0])


def per_device(first_view, second_view):
    row_count, feature_width = first_view.shape
    chunks = feature_width // (NZ * LANES)
    width = chunks * LANES
    rows = row_count * NZ
    total_rows = rows * PLANE
    half = feature_width // CORES
    bf16, f32 = jnp.bfloat16, jnp.float32
    views = [
        view.reshape(row_count, feature_width // LANES, LANES).transpose(1, 0, 2)
        for view in (first_view, second_view)
    ]
    grads = pl.pallas_call(
        kernel,
        out_shape=jax.ShapeDtypeStruct((2, half // LANES, row_count, LANES), bf16),
        in_specs=[pl.BlockSpec(memory_space=pltpu.HBM)] * 2,
        out_specs=pl.BlockSpec(memory_space=pltpu.VMEM),
        scratch_shapes=[
            pltpu.VMEM((feature_width // LANES, row_count, LANES), bf16),
            pltpu.VMEM((chunks, NZ, row_count, LANES), bf16),
            pltpu.VMEM((PLANE, chunks, NZ, row_count, LANES), bf16),
            pltpu.VMEM((PLANE, rows, width), bf16),
            pltpu.VMEM((PLANE, rows, width), bf16),
            pltpu.VMEM((rows, total_rows), bf16),
            pltpu.VMEM((NZ, rows, total_rows), bf16),
            pltpu.VMEM((chunks, LANES), f32),
            pltpu.VMEM((PLANE, chunks, LANES), f32),
            pltpu.VMEM((chunks, NZ, row_count, LANES), bf16),
            pltpu.SemaphoreType.DMA,
            pltpu.SemaphoreType.DMA((NZ,)),
            pltpu.SemaphoreType.DMA((7,)),
            pltpu.SemaphoreType.DMA((8,)),
        ],
        compiler_params=pltpu.CompilerParams(
            collective_id=0, has_side_effects=True, vmem_limit_bytes=32 << 20
        ),
        name="twins",
    )(*[pltpu.with_memory_space_constraint(view, pltpu.HBM) for view in views])
    return tuple(grads[v].transpose(1, 0, 2).reshape(row_count, half) for v in range(2))


def solution(mesh):
    return jax.shard_map(
        per_device,
        mesh=mesh,
        in_specs=(P("batch", None), P("batch", None)),
        out_specs=(P("batch", "tile"), P("batch", "tile")),
        check_vma=False,
    )
```

```python
import jax
import jax.numpy as jnp
from jax import lax
from jax.experimental import pallas as pl
from jax.experimental.pallas import tpu as pltpu
from jax.sharding import PartitionSpec as P

epsilon = 1e-05
decorrelation = 0.0051

NY, NZ, NX = 4, 8, 4
PLANE = NY * NX
CORES = 2
LANES = 128
MESH = pl.DeviceIdType.MESH


def fold(values):
    while values.shape[0] > 8:
        half = values.shape[0] // 2
        values = values[:half] + values[half:]
    return jnp.sum(values, 0, keepdims=True)


def kernel(
    first_ref,
    second_ref,
    grads_ref,
    stage,
    line,
    whole,
    norm,
    other,
    gram_out,
    gram_in,
    stat_out,
    stat_in,
    grad_out,
    load_sem,
    line_sem,
    send_sem,
    recv_sem,
):
    batch = lax.axis_index("batch")
    tile = lax.axis_index("tile")
    x = batch % NX
    z = (batch // NX) % NZ
    y = batch // (NX * NZ)
    slot = y * NX + x
    chunks, pair = line.shape[0], line.shape[2]
    rows = NZ * pair
    total_rows = rows * PLANE
    whole_rows = whole.reshape(PLANE, chunks, rows, LANES)
    grad_rows = grad_out.reshape(chunks, rows, LANES)

    def line_peer(k):
        return (y * NZ + (z + k) % NZ) * NX + x

    def plane_peer(j, i):
        return (((y + j) % NY) * NZ + z) * NX + (x + i) % NX

    def block_of(k):
        turned = (k + 1) % NZ
        return (turned + NZ // 2) % NZ

    line_steps = [4, 3, 5, 2, 6, 1, 7]
    plane_steps = [(j, i) for j in (2, 1, 3, 0) for i in (2, 1, 3, 0) if i or j]
    far_steps = [(j, i) for j, i in plane_steps if min(j, NY - j) + min(i, NX - i) > 2]
    near_steps = [step for step in plane_steps if step not in far_steps]
    sibling = (batch, 1 - tile)

    barrier = pltpu.get_barrier_semaphore()
    greeted = [(line_peer(k), tile) for k in line_steps]
    greeted += [(plane_peer(j, i), tile) for j, i in plane_steps] + [sibling]
    for device in greeted:
        pl.semaphore_signal(barrier, inc=1, device_id=device, device_id_type=MESH)
    @pl.when(tile == 0)
    def _():
        pltpu.make_async_copy(first_ref, stage, load_sem).start()

    @pl.when(tile == 1)
    def _():
        pltpu.make_async_copy(second_ref, stage, load_sem).start()

    pltpu.make_async_copy(stage, stage, load_sem).wait()
    own = stage.at[pl.ds(block_of(z) * chunks, chunks)]
    pltpu.make_async_copy(own, line.at[:, z], line_sem.at[0]).start()
    pl.semaphore_wait(barrier, len(greeted))

    def send(phase, source, target, device, arrived=None):
        pltpu.make_async_remote_copy(
            src_ref=source,
            dst_ref=target,
            send_sem=send_sem.at[phase],
            recv_sem=recv_sem.at[phase] if arrived is None else arrived,
            device_id=device,
            device_id_type=MESH,
        ).start()

    def wait(sem, like):
        pltpu.make_async_copy(like, like, sem).wait()

    for k in line_steps:
        source = stage.at[pl.ds(block_of((z + k) % NZ) * chunks, chunks)]
        send(0, source, line.at[:, z], (line_peer(k), tile), line_sem.at[k])
    @pl.loop(0, NZ)
    def _(n):
        k = jnp.where(n % 2 == 1, (n + 1) // 2, (NZ - n // 2) % NZ)
        origin = (z + NZ - k) % NZ
        piece = line.at[:, origin]
        wait(line_sem.at[k], piece)
        for j, i in plane_steps:
            send(
                1,
                piece,
                whole.at[slot, :, origin],
                (plane_peer(j, i), tile),
                recv_sem.at[6 if (j, i) in far_steps else 1],
            )

    line_rows = line.reshape(chunks, rows, LANES)
    shifts = [
        jnp.sum(line_rows[c].astype(jnp.float32), 0, keepdims=True) / rows for c in range(chunks)
    ]
    sums = [jnp.zeros((8, LANES), jnp.float32)] * chunks
    squares = [jnp.zeros((8, LANES), jnp.float32)] * chunks

    def gather(source, block_rows):
        for c in range(chunks):
            block = block_rows[c]
            norm[source, :, c * LANES : (c + 1) * LANES] = block
            values = block.astype(jnp.float32) - shifts[c]
            sums[c] += values[:8] + values[8:]
            squares[c] += values[:8] * values[:8] + values[8:] * values[8:]

    gather(slot, line_rows)
    for sem, steps in ((1, near_steps), (6, far_steps)):
        wait(recv_sem.at[sem], whole.at[pl.ds(0, len(steps))])
        for j, i in steps:
            source = (y + NY - j) % NY * NX + (x + NX - i) % NX
            gather(source, whole_rows.at[source])
    moves = [jnp.sum(v, 0, keepdims=True) / total_rows for v in sums]
    means = [s + m for s, m in zip(shifts, moves)]
    inverse = [
        lax.rsqrt(jnp.sum(v, 0, keepdims=True) / total_rows - m * m + epsilon)
        for v, m in zip(squares, moves)
    ]
    def normalized(values, c):
        return ((values.astype(jnp.float32) - means[c]) * inverse[c]).astype(jnp.bfloat16)

    width = chunks * LANES
    gram, mine = jnp.zeros((rows, total_rows), jnp.float32), []
    for c in range(0, chunks, 2):
        pair_rows = []
        for d in (c, c + 1):
            lanes = slice(d * LANES, (d + 1) * LANES)
            values = normalized(norm[:, :, lanes].reshape(total_rows, LANES), d)
            norm[:, :, lanes] = values.reshape(PLANE, rows, LANES)
            pair_rows.append(values)
            mine.append(normalized(line_rows[d], d))
        gram += lax.dot_general(
            jnp.concatenate(mine[-2:], 1),
            jnp.concatenate(pair_rows, 1),
            (((1,), (1,)), ((), ())),
            preferred_element_type=jnp.float32,
        )
    inverse = jnp.concatenate(inverse, 1)
    mine = jnp.concatenate(mine, 1).astype(jnp.float32)
    gram_out[...] = gram.astype(jnp.bfloat16)

    for k in line_steps:
        send(2, gram_out, gram_in.at[z], (line_peer(k), 1 - tile))
    send(2, gram_out, gram_in.at[z], sibling)
    send(3, norm, other, sibling)
    wait(recv_sem.at[3], other)
    paired = []
    for c in range(chunks):
        lanes = slice(c * LANES, (c + 1) * LANES)
        product = norm[:, :, lanes].astype(jnp.float32) * other[:, :, lanes].astype(jnp.float32)
        paired.append(fold(product.reshape(total_rows, LANES)))
    paired = jnp.concatenate(paired, 1) / total_rows
    excess = (paired - 1.0) - decorrelation * paired
    direct = excess * other[slot].astype(jnp.float32)
    wait(recv_sem.at[2], gram_in)
    gram = jnp.sum(gram_in[...].astype(jnp.float32), 0) * (decorrelation / total_rows)
    high = gram.astype(jnp.bfloat16)
    low = (gram - high.astype(jnp.float32)).astype(jnp.bfloat16)
    both = jnp.dot(
        jnp.concatenate([high, low], 0),
        norm[...].reshape(total_rows, width),
        preferred_element_type=jnp.float32,
    )
    pull = both[:rows] + both[rows:] + direct
    stat = fold(pull * mine)
    for c in range(chunks):
        stat_out[c : c + 1] = stat[:, c * LANES : (c + 1) * LANES]

    for j, i in plane_steps:
        arrived = recv_sem.at[5 if (j, i) in far_steps else 4]
        send(4, stat_out, stat_in.at[slot], (plane_peer(j, i), tile), arrived)
    scaled_pull, scaled_mine = inverse * pull, inverse * mine
    stat = stat_out[...]
    for sem, steps in ((4, near_steps), (5, far_steps)):
        wait(recv_sem.at[sem], stat_in.at[pl.ds(0, len(steps))])
        for j, i in steps:
            stat += stat_in[(y + NY - j) % NY * NX + (x + NX - i) % NX]
    stat = stat / total_rows
    for c in range(chunks):
        lanes = slice(c * LANES, (c + 1) * LANES)
        grad = scaled_pull[:, lanes] - scaled_mine[:, lanes] * stat[c : c + 1]
        grad_rows[c] = grad.astype(jnp.bfloat16)

    owner = block_of(z) // (NZ // CORES)
    target = grads_ref.at[tile, pl.ds(block_of(z) % (NZ // CORES) * chunks, chunks)]
    for k in line_steps:
        send(5, grad_out.at[:, (z + k) % NZ], target, (line_peer(k), owner), recv_sem.at[7])

    @pl.when(owner == tile)
    def _():
        pltpu.make_async_copy(grad_out.at[:, z], target, recv_sem.at[7]).start()

    @pl.when(owner != tile)
    def _():
        send(6, grad_out.at[:, z], target, sibling, recv_sem.at[7])

    wait(recv_sem.at[7], grads_ref)

    wait(send_sem.at[0], line.at[:, pl.ds(0, NZ - 1)])
    wait(send_sem.at[1], whole.at[pl.ds(0, PLANE - 1)])
    wait(send_sem.at[2], gram_in)
    wait(send_sem.at[3], other)
    wait(send_sem.at[4], stat_in.at[pl.ds(0, PLANE - 1)])
    wait(send_sem.at[5], grad_out.at[:, pl.ds(0, NZ - 1)])

    @pl.when(owner != tile)
    def _():
        wait(send_sem.at[6], grad_out.at[:, 0])


def per_device(first_view, second_view):
    row_count, feature_width = first_view.shape
    chunks = feature_width // (NZ * LANES)
    width = chunks * LANES
    rows = row_count * NZ
    total_rows = rows * PLANE
    half = feature_width // CORES
    bf16, f32 = jnp.bfloat16, jnp.float32
    views = [
        view.reshape(row_count, feature_width // LANES, LANES).transpose(1, 0, 2)
        for view in (first_view, second_view)
    ]
    grads = pl.pallas_call(
        kernel,
        out_shape=jax.ShapeDtypeStruct((2, half // LANES, row_count, LANES), bf16),
        in_specs=[pl.BlockSpec(memory_space=pltpu.HBM)] * 2,
        out_specs=pl.BlockSpec(memory_space=pltpu.VMEM),
        scratch_shapes=[
            pltpu.VMEM((feature_width // LANES, row_count, LANES), bf16),
            pltpu.VMEM((chunks, NZ, row_count, LANES), bf16),
            pltpu.VMEM((PLANE, chunks, NZ, row_count, LANES), bf16),
            pltpu.VMEM((PLANE, rows, width), bf16),
            pltpu.VMEM((PLANE, rows, width), bf16),
            pltpu.VMEM((rows, total_rows), bf16),
            pltpu.VMEM((NZ, rows, total_rows), bf16),
            pltpu.VMEM((chunks, LANES), f32),
            pltpu.VMEM((PLANE, chunks, LANES), f32),
            pltpu.VMEM((chunks, NZ, row_count, LANES), bf16),
            pltpu.SemaphoreType.DMA,
            pltpu.SemaphoreType.DMA((NZ,)),
            pltpu.SemaphoreType.DMA((7,)),
            pltpu.SemaphoreType.DMA((8,)),
        ],
        compiler_params=pltpu.CompilerParams(
            collective_id=0, has_side_effects=True, vmem_limit_bytes=32 << 20
        ),
        name="twins",
    )(*[pltpu.with_memory_space_constraint(view, pltpu.HBM) for view in views])
    return tuple(grads[v].transpose(1, 0, 2).reshape(row_count, half) for v in range(2))


def solution(mesh):
    return jax.shard_map(
        per_device,
        mesh=mesh,
        in_specs=(P("batch", None), P("batch", None)),
        out_specs=(P("batch", "tile"), P("batch", "tile")),
        check_vma=False,
    )
```

```python
import jax
import jax.numpy as jnp
from jax import lax
from jax.experimental import pallas as pl
from jax.experimental.pallas import tpu as pltpu
from jax.sharding import PartitionSpec as P

epsilon = 1e-05
decorrelation = 0.0051

NY, NZ, NX = 4, 8, 4
PLANE = NY * NX
CORES = 2
LANES = 128
MESH = pl.DeviceIdType.MESH


def fold(values):
    while values.shape[0] > 8:
        half = values.shape[0] // 2
        values = values[:half] + values[half:]
    return jnp.sum(values, 0, keepdims=True)


def kernel(
    first_ref,
    second_ref,
    grads_ref,
    stage,
    line,
    whole,
    norm,
    other,
    gram_out,
    gram_in,
    stat_out,
    stat_in,
    grad_out,
    load_sem,
    line_sem,
    send_sem,
    recv_sem,
):
    batch = lax.axis_index("batch")
    tile = lax.axis_index("tile")
    x = batch % NX
    z = (batch // NX) % NZ
    y = batch // (NX * NZ)
    slot = y * NX + x
    chunks, pair = line.shape[0], line.shape[2]
    rows = NZ * pair
    total_rows = rows * PLANE
    whole_rows = whole.reshape(PLANE, chunks, rows, LANES)
    grad_rows = grad_out.reshape(chunks, rows, LANES)

    def line_peer(k):
        return (y * NZ + (z + k) % NZ) * NX + x

    def plane_peer(j, i):
        return (((y + j) % NY) * NZ + z) * NX + (x + i) % NX

    def block_of(k):
        turned = (k + 1) % NZ
        return (turned + NZ // 2) % NZ

    line_steps = [4, 3, 5, 2, 6, 1, 7]
    plane_steps = [(j, i) for j in (2, 1, 3, 0) for i in (2, 1, 3, 0) if i or j]
    plane_steps.sort(key=lambda s: -min(s[0], NY - s[0]) - min(s[1], NX - s[1]))
    far_steps = [(j, i) for j, i in plane_steps if min(j, NY - j) + min(i, NX - i) > 2]
    near_steps = [step for step in plane_steps if step not in far_steps]
    sibling = (batch, 1 - tile)

    barrier = pltpu.get_barrier_semaphore()
    greeted = [(line_peer(k), tile) for k in line_steps]
    greeted += [(plane_peer(j, i), tile) for j, i in plane_steps] + [sibling]
    for device in greeted:
        pl.semaphore_signal(barrier, inc=1, device_id=device, device_id_type=MESH)
    @pl.when(tile == 0)
    def _():
        pltpu.make_async_copy(first_ref, stage, load_sem).start()

    @pl.when(tile == 1)
    def _():
        pltpu.make_async_copy(second_ref, stage, load_sem).start()

    pltpu.make_async_copy(stage, stage, load_sem).wait()
    own = stage.at[pl.ds(block_of(z) * chunks, chunks)]
    pltpu.make_async_copy(own, line.at[:, z], line_sem.at[0]).start()
    pl.semaphore_wait(barrier, len(greeted))

    def send(phase, source, target, device, arrived=None):
        pltpu.make_async_remote_copy(
            src_ref=source,
            dst_ref=target,
            send_sem=send_sem.at[phase],
            recv_sem=recv_sem.at[phase] if arrived is None else arrived,
            device_id=device,
            device_id_type=MESH,
        ).start()

    def wait(sem, like):
        pltpu.make_async_copy(like, like, sem).wait()

    for k in line_steps:
        source = stage.at[pl.ds(block_of((z + k) % NZ) * chunks, chunks)]
        send(0, source, line.at[:, z], (line_peer(k), tile), line_sem.at[k])
    @pl.loop(0, NZ)
    def _(n):
        k = jnp.where(n % 2 == 1, (n + 1) // 2, (NZ - n // 2) % NZ)
        origin = (z + NZ - k) % NZ
        piece = line.at[:, origin]
        wait(line_sem.at[k], piece)
        for j, i in plane_steps:
            send(
                1,
                piece,
                whole.at[slot, :, origin],
                (plane_peer(j, i), tile),
                recv_sem.at[6 if (j, i) in far_steps else 1],
            )

    line_rows = line.reshape(chunks, rows, LANES)
    shifts = [
        jnp.sum(line_rows[c].astype(jnp.float32), 0, keepdims=True) / rows for c in range(chunks)
    ]
    sums = [jnp.zeros((8, LANES), jnp.float32)] * chunks
    squares = [jnp.zeros((8, LANES), jnp.float32)] * chunks

    def gather(source, block_rows):
        for c in range(chunks):
            block = block_rows[c]
            norm[source, :, c * LANES : (c + 1) * LANES] = block
            values = block.astype(jnp.float32) - shifts[c]
            sums[c] += values[:8] + values[8:]
            squares[c] += values[:8] * values[:8] + values[8:] * values[8:]

    gather(slot, line_rows)
    for sem, steps in ((1, near_steps), (6, far_steps)):
        wait(recv_sem.at[sem], whole.at[pl.ds(0, len(steps))])
        for j, i in steps:
            source = (y + NY - j) % NY * NX + (x + NX - i) % NX
            gather(source, whole_rows.at[source])
    moves = [jnp.sum(v, 0, keepdims=True) / total_rows for v in sums]
    means = [s + m for s, m in zip(shifts, moves)]
    inverse = [
        lax.rsqrt(jnp.sum(v, 0, keepdims=True) / total_rows - m * m + epsilon)
        for v, m in zip(squares, moves)
    ]
    def normalized(values, c):
        return ((values.astype(jnp.float32) - means[c]) * inverse[c]).astype(jnp.bfloat16)

    width = chunks * LANES
    gram, mine = jnp.zeros((rows, total_rows), jnp.float32), []
    for c in range(0, chunks, 2):
        pair_rows = []
        for d in (c, c + 1):
            lanes = slice(d * LANES, (d + 1) * LANES)
            values = normalized(norm[:, :, lanes].reshape(total_rows, LANES), d)
            norm[:, :, lanes] = values.reshape(PLANE, rows, LANES)
            pair_rows.append(values)
            mine.append(normalized(line_rows[d], d))
        gram += lax.dot_general(
            jnp.concatenate(mine[-2:], 1),
            jnp.concatenate(pair_rows, 1),
            (((1,), (1,)), ((), ())),
            preferred_element_type=jnp.float32,
        )
    inverse = jnp.concatenate(inverse, 1)
    mine = jnp.concatenate(mine, 1).astype(jnp.float32)
    gram_out[...] = gram.astype(jnp.bfloat16)

    for k in line_steps:
        send(2, gram_out, gram_in.at[z], (line_peer(k), 1 - tile))
    send(2, gram_out, gram_in.at[z], sibling)
    send(3, norm, other, sibling)
    wait(recv_sem.at[3], other)
    paired = []
    for c in range(chunks):
        lanes = slice(c * LANES, (c + 1) * LANES)
        product = norm[:, :, lanes].astype(jnp.float32) * other[:, :, lanes].astype(jnp.float32)
        paired.append(fold(product.reshape(total_rows, LANES)))
    paired = jnp.concatenate(paired, 1) / total_rows
    excess = (paired - 1.0) - decorrelation * paired
    direct = excess * other[slot].astype(jnp.float32)
    wait(recv_sem.at[2], gram_in)
    gram = jnp.sum(gram_in[...].astype(jnp.float32), 0) * (decorrelation / total_rows)
    high = gram.astype(jnp.bfloat16)
    low = (gram - high.astype(jnp.float32)).astype(jnp.bfloat16)
    both = jnp.dot(
        jnp.concatenate([high, low], 0),
        norm[...].reshape(total_rows, width),
        preferred_element_type=jnp.float32,
    )
    pull = both[:rows] + both[rows:] + direct
    stat = fold(pull * mine)
    for c in range(chunks):
        stat_out[c : c + 1] = stat[:, c * LANES : (c + 1) * LANES]

    for j, i in plane_steps:
        arrived = recv_sem.at[5 if (j, i) in far_steps else 4]
        send(4, stat_out, stat_in.at[slot], (plane_peer(j, i), tile), arrived)
    scaled_pull, scaled_mine = inverse * pull, inverse * mine
    stat = stat_out[...]
    for sem, steps in ((4, near_steps), (5, far_steps)):
        wait(recv_sem.at[sem], stat_in.at[pl.ds(0, len(steps))])
        for j, i in steps:
            stat += stat_in[(y + NY - j) % NY * NX + (x + NX - i) % NX]
    stat = stat / total_rows
    for c in range(chunks):
        lanes = slice(c * LANES, (c + 1) * LANES)
        grad = scaled_pull[:, lanes] - scaled_mine[:, lanes] * stat[c : c + 1]
        grad_rows[c] = grad.astype(jnp.bfloat16)

    owner = block_of(z) // (NZ // CORES)
    target = grads_ref.at[tile, pl.ds(block_of(z) % (NZ // CORES) * chunks, chunks)]
    for k in line_steps:
        send(5, grad_out.at[:, (z + k) % NZ], target, (line_peer(k), owner), recv_sem.at[7])

    @pl.when(owner == tile)
    def _():
        pltpu.make_async_copy(grad_out.at[:, z], target, recv_sem.at[7]).start()

    @pl.when(owner != tile)
    def _():
        send(6, grad_out.at[:, z], target, sibling, recv_sem.at[7])

    wait(recv_sem.at[7], grads_ref)

    wait(send_sem.at[0], line.at[:, pl.ds(0, NZ - 1)])
    wait(send_sem.at[1], whole.at[pl.ds(0, PLANE - 1)])
    wait(send_sem.at[2], gram_in)
    wait(send_sem.at[3], other)
    wait(send_sem.at[4], stat_in.at[pl.ds(0, PLANE - 1)])
    wait(send_sem.at[5], grad_out.at[:, pl.ds(0, NZ - 1)])

    @pl.when(owner != tile)
    def _():
        wait(send_sem.at[6], grad_out.at[:, 0])


def per_device(first_view, second_view):
    row_count, feature_width = first_view.shape
    chunks = feature_width // (NZ * LANES)
    width = chunks * LANES
    rows = row_count * NZ
    total_rows = rows * PLANE
    half = feature_width // CORES
    bf16, f32 = jnp.bfloat16, jnp.float32
    views = [
        view.reshape(row_count, feature_width // LANES, LANES).transpose(1, 0, 2)
        for view in (first_view, second_view)
    ]
    grads = pl.pallas_call(
        kernel,
        out_shape=jax.ShapeDtypeStruct((2, half // LANES, row_count, LANES), bf16),
        in_specs=[pl.BlockSpec(memory_space=pltpu.HBM)] * 2,
        out_specs=pl.BlockSpec(memory_space=pltpu.VMEM),
        scratch_shapes=[
            pltpu.VMEM((feature_width // LANES, row_count, LANES), bf16),
            pltpu.VMEM((chunks, NZ, row_count, LANES), bf16),
            pltpu.VMEM((PLANE, chunks, NZ, row_count, LANES), bf16),
            pltpu.VMEM((PLANE, rows, width), bf16),
            pltpu.VMEM((PLANE, rows, width), bf16),
            pltpu.VMEM((rows, total_rows), bf16),
            pltpu.VMEM((NZ, rows, total_rows), bf16),
            pltpu.VMEM((chunks, LANES), f32),
            pltpu.VMEM((PLANE, chunks, LANES), f32),
            pltpu.VMEM((chunks, NZ, row_count, LANES), bf16),
            pltpu.SemaphoreType.DMA,
            pltpu.SemaphoreType.DMA((NZ,)),
            pltpu.SemaphoreType.DMA((7,)),
            pltpu.SemaphoreType.DMA((8,)),
        ],
        compiler_params=pltpu.CompilerParams(
            collective_id=0, has_side_effects=True, vmem_limit_bytes=32 << 20
        ),
        name="twins",
    )(*[pltpu.with_memory_space_constraint(view, pltpu.HBM) for view in views])
    return tuple(grads[v].transpose(1, 0, 2).reshape(row_count, half) for v in range(2))


def solution(mesh):
    return jax.shard_map(
        per_device,
        mesh=mesh,
        in_specs=(P("batch", None), P("batch", None)),
        out_specs=(P("batch", "tile"), P("batch", "tile")),
        check_vma=False,
    )
```
